512 devices in a mesh: gx: 4 (over x_lo, core), gy: 8 (over x_hi, y), gz: 16 (over z).
Axes of the slice: x: 4 (x_hi: 2, x_lo: 2; x = x_hi * 2 + x_lo), y: 4, z: 16, core: 2. Of those that a mesh axis runs over, the one named last changes fastest.
Arguments:
- density: float32 [128, 256, 2048], P('gz', 'gx', 'gy'), may hold values from 0.2 to 2
- bins: int32 [128, 256, 2048], P('gz', 'gx', 'gy'), may hold values from 0 to 255
- colour_table: bfloat16 [3, 256], replicated, may hold values from 0.049804688 to 1
- opacity_table: bfloat16 [256], replicated, may hold values from 0.19921875 to 2.5
- order: int32 [4, 8, 16], P('gx', 'gy'), may hold values from 0 to 15, each once within a row
Outputs:
- image: float32 [4, 256, 2048], P(None, ('gx', 'gz'), 'gy')
The draws below stay inside these ranges and needn't reach their ends.
Inputs may be any that keep to these rules, and one draw needn't show every extreme that they name: For each column block and row block, order holds each brick rank 0 to 15 once.
All inputs are finite; a program needn't handle non-finite values.
Results may differ from the reference program's by a relative error of at most 0.0003.
Values sent between devices are 32-bit elements; how exact they have to be, the bound alone decides.
A program may use at most 64 MiB of HBM per device.

```python
import math
import jax
import jax.numpy as jnp
from jax import lax

KBINS = 256
BX = 64
BY = 256
BZ = 8
NX = 256
NY = 2048
NZ = 128
N_GX = 4
N_GY = 8
N_GZ = 16


def with_ends(result, own_key, least, largest):
    extent = result.shape
    place = [jax.random.randint(jax.random.fold_in(own_key, axis), (), 0, extent[axis]) for axis in range(len(extent))]
    result = result.at[tuple(place)].set(least)
    longest = extent.index(max(extent))
    place[longest] = (place[longest] + 1) % extent[longest]
    return result.at[tuple(place)].set(largest)


def levels(stream_key, shape, pieces, low, top_value):
    def one(position, shards_of):
        steps = jax.random.uniform(jax.random.fold_in(jax.random.fold_in(stream_key, 6), position), (shards_of,), jnp.float32, low / len(pieces), top_value / len(pieces))
        return jnp.repeat(jnp.exp(steps), shape[position] // shards_of).reshape((-1,) + (1,) * (len(shape) - position - 1))

    level = one(*pieces[0])
    for cut in pieces[1:]:
        level = level * one(*cut)
    return level


def setup_inputs(seed: int = 0) -> dict:
    key_of = jax.random.split(jax.random.key(seed), 6)
    return {
        "density": jnp.clip(jnp.exp(math.log(2.0) - 2.3025851 * jax.random.uniform(key_of[0], (NZ, NX, NY), jnp.float32) ** levels(key_of[0], (NZ, NX, NY), ((0, 16), (1, 4), (2, 8)), -0.2, 0.2)), 0.2, 2.0),
        "bins": with_ends(jax.random.randint(key_of[1], (NZ, NX, NY), 0, KBINS), jax.random.fold_in(key_of[1], 1), 0, KBINS - 1).astype(jnp.int32),
        "colour_table": jnp.clip(jax.random.uniform(key_of[2], (3, KBINS), jnp.float32, 0.049804688, 1.0), 0.049804688, 1.0).astype(jnp.bfloat16),
        "opacity_table": jnp.clip(jnp.exp(jax.random.uniform(key_of[3], (KBINS,), jnp.float32, math.log(0.19921875), math.log(2.5))), 0.19921875, 2.5).astype(jnp.bfloat16),
        "order": jax.vmap(lambda own: jax.random.permutation(own, N_GZ))(jax.random.split(key_of[4], N_GX * N_GY)).reshape((N_GX, N_GY, N_GZ)).astype(jnp.int32),
    }


def reference(density, bins, colour_table, opacity_table, order):
    padded = jnp.pad(density, 1)
    slope_depth = (padded[2:, 1:-1, 1:-1] - padded[:-2, 1:-1, 1:-1]) * 0.5
    slope_column = (padded[1:-1, 2:, 1:-1] - padded[1:-1, :-2, 1:-1]) * 0.5
    slope_row = (padded[1:-1, 1:-1, 2:] - padded[1:-1, 1:-1, :-2]) * 0.5
    facing = 0.64 * slope_depth + 0.48 * slope_column + 0.6 * slope_row
    length = jnp.sqrt(slope_depth * slope_depth + slope_column * slope_column + slope_row * slope_row + 1.0)
    shade = 0.25 + 0.75 * jnp.abs(facing) / length
    opacity = opacity_table.astype(jnp.float32)[bins]
    sigma = opacity * density * (3.0 / NZ)
    alpha = 1.0 - jnp.exp(-sigma)
    sigma_bricks = sigma.reshape(N_GZ, BZ, NX, NY)
    excl = jnp.cumsum(sigma_bricks, axis=1) - sigma_bricks
    weight = jnp.exp(-excl) * alpha.reshape(N_GZ, BZ, NX, NY) * shade.reshape(N_GZ, BZ, NX, NY)
    brick_depth = lax.optimization_barrier(jnp.sum(sigma_bricks, axis=1))
    earlier = (order[:, :, None, :] < order[:, :, :, None]).astype(jnp.float32)
    split_depth = brick_depth.reshape(N_GZ, N_GX, BX, N_GY, BY)
    prefix = jnp.einsum('uvab,buxvy->auxvy', earlier, split_depth, precision=lax.Precision.HIGHEST)
    attenuation = jnp.exp(-prefix.reshape(N_GZ, NX, NY))
    channels = []
    for channel in range(3):
        colour = colour_table[channel].astype(jnp.float32)[bins].reshape(N_GZ, BZ, NX, NY)
        brick_colour = lax.optimization_barrier(jnp.sum(weight * colour, axis=1))
        channels.append(lax.optimization_barrier(jnp.sum(attenuation * brick_colour, axis=0)))
    channels.append(1.0 - jnp.exp(-lax.optimization_barrier(jnp.sum(brick_depth, axis=0))))
    return jnp.stack(channels, axis=0)
```

```python
import functools
import math

import jax
import jax.numpy as jnp
from jax import lax
from jax.experimental import pallas as pl
from jax.experimental.pallas import tpu as pltpu
from jax.sharding import PartitionSpec as P

MESH = pl.DeviceIdType.MESH
LANES = 128
ROWS = 8
F32 = jnp.float32


def kernel(
    n_z,
    scale,
    dens_hbm,
    bins_hbm,
    ctab_ref,
    otab_ref,
    order_ref,
    out_ref,
    dens,
    bins,
    tabs,
    weight,
    edge,
    halo,
    send,
    recv,
    inv,
    load_sem,
    halo_send,
    halo_recv,
    tile_send,
    tile_recv,
    known,
):
    gx, gy, me = lax.axis_index("gx"), lax.axis_index("gy"), lax.axis_index("gz")
    n_x, n_y = lax.axis_size("gx"), lax.axis_size("gy")
    depth, _, height, _ = bins.shape
    blocks = height // ROWS

    def step(index, count, by):
        return lax.rem(index + (by + count), count)

    neighbours = [
        {"gx": step(gx, n_x, -1)},
        {"gx": step(gx, n_x, 1)},
        {"gy": step(gy, n_y, -1)},
        {"gy": step(gy, n_y, 1)},
        {"gz": step(me, n_z, -1)},
        {"gz": step(me, n_z, 1)},
    ]

    loads = []
    for half in range(2):
        lanes = pl.ds(half * LANES, LANES)
        loads.append(
            pltpu.make_async_copy(
                dens_hbm.at[:, :, lanes],
                dens.at[pl.ds(1, depth), half, pl.ds(ROWS, height), :],
                load_sem.at[half],
            )
        )
    for half in range(2):
        lanes = pl.ds(half * LANES, LANES)
        loads.append(
            pltpu.make_async_copy(
                bins_hbm.at[:, :, lanes], bins.at[:, half], load_sem.at[2 + half]
            )
        )
    for load in loads:
        load.start()

    barrier = pltpu.get_barrier_semaphore()
    for other in neighbours:
        pl.semaphore_signal(barrier, inc=1, device_id=other, device_id_type=MESH)

    table = jnp.concatenate(
        [ctab_ref[...].astype(F32), otab_ref[...].astype(F32) * scale], axis=0
    )
    for c in range(4):
        for half in range(2):
            row = table[c : c + 1, half * LANES : (half + 1) * LANES]
            tabs[c, half] = jnp.broadcast_to(row, (ROWS, LANES))

    pl.semaphore_wait(barrier, len(neighbours))

    def greet(level):
        for sign in (-1, 1):
            pl.semaphore_signal(
                known.at[level],
                inc=1,
                device_id={"gz": step(me, n_z, sign * (1 << level))},
                device_id_type=MESH,
            )

    greet(0)
    loads[0].wait()
    loads[1].wait()

    def remote(src, dst, index, other):
        return pltpu.make_async_remote_copy(
            src_ref=src,
            dst_ref=dst,
            send_sem=halo_send.at[index],
            recv_sem=halo_recv.at[index],
            device_id=other,
            device_id_type=MESH,
        )

    own_rows = pl.ds(ROWS, height)
    own_planes = pl.ds(1, depth)
    z_up = remote(
        dens.at[depth, :, own_rows, :], dens.at[0, :, own_rows, :], 0, neighbours[5]
    )
    z_down = remote(
        dens.at[1, :, own_rows, :],
        dens.at[depth + 1, :, own_rows, :],
        1,
        neighbours[4],
    )
    x_up = remote(
        dens.at[own_planes, :, pl.ds(height, ROWS), :],
        dens.at[own_planes, :, pl.ds(0, ROWS), :],
        2,
        neighbours[1],
    )
    x_down = remote(
        dens.at[own_planes, :, pl.ds(ROWS, ROWS), :],
        dens.at[own_planes, :, pl.ds(height + ROWS, ROWS), :],
        3,
        neighbours[0],
    )
    copies = [z_up, z_down, x_up, x_down]
    for copy in copies:
        copy.start()

    lane = lax.broadcasted_iota(jnp.int32, (ROWS, LANES), 1)
    sub = lax.broadcasted_iota(jnp.int32, (ROWS, LANES), 0)

    first = jnp.zeros((ROWS, LANES), F32)
    last = jnp.zeros((ROWS, LANES), F32)
    for z in range(depth):
        for b in range(blocks):
            k = z * blocks + b
            rows = pl.ds(ROWS + b * ROWS, ROWS)
            first = jnp.where(
                lane == k, jnp.broadcast_to(dens[z + 1, 0, rows, 0:1], first.shape), first
            )
            last = jnp.where(
                lane == k,
                jnp.broadcast_to(dens[z + 1, 1, rows, LANES - 1 : LANES], last.shape),
                last,
            )
    edge[0] = first
    edge[1] = last
    y_up = remote(edge.at[1], halo.at[0], 4, neighbours[3])
    y_down = remote(edge.at[0], halo.at[1], 5, neighbours[2])
    y_up.start()
    y_down.start()
    copies += [y_up, y_down]

    pl.semaphore_wait(known.at[0], 2)
    greet(1)

    def split(block, channel, low, high):
        send[2 * block, channel] = jnp.where(sub < 4, low, pltpu.roll(high, 4, 0))
        send[2 * block + 1, channel] = jnp.where(sub < 4, pltpu.roll(low, 4, 0), high)

    def looked(c, index, upper):
        return jnp.where(
            upper,
            jnp.take_along_axis(tabs[c, 1], index, axis=1, mode="promise_in_bounds"),
            jnp.take_along_axis(tabs[c, 0], index, axis=1, mode="promise_in_bounds"),
        )

    loads[2].wait()
    loads[3].wait()

    def optical(block, carry):
        rows = pl.ds(pl.multiple_of(block * ROWS, ROWS), ROWS)
        padded = pl.ds(pl.multiple_of(block * ROWS + ROWS, ROWS), ROWS)
        ends = []
        for half in range(2):
            total = jnp.zeros((ROWS, LANES), F32)
            before = jnp.ones((ROWS, LANES), F32)
            for z in range(depth):
                bin_ = bins[z, half, rows, :]
                sigma = looked(3, bin_ & (LANES - 1), bin_ >= LANES)
                total = total + sigma * dens[z + 1, half, padded, :]
                after = jnp.exp2(total)
                weight[z, half, rows, :] = before - after
                before = after
            ends.append(total)
        split(block, 3, *ends)
        return carry

    lax.fori_loop(0, blocks, optical, 0)

    pl.semaphore_wait(known.at[1], 2)
    greet(2)

    def place(rank, carry):
        slot = jnp.int32(0)
        for b in range(n_z):
            here = lax.rem(me + (n_z - b), n_z)
            slot = jnp.where(order_ref[0, 0, b] == rank, here, slot)
        inv[rank] = slot
        return carry

    lax.fori_loop(0, n_z, place, 0)

    for copy in copies:
        copy.wait_recv()

    blank = jnp.zeros((ROWS, LANES), F32)

    @pl.when(gx == 0)
    def _():
        for z in range(depth):
            for half in range(2):
                dens[z + 1, half, pl.ds(0, ROWS), :] = blank

    @pl.when(gx == n_x - 1)
    def _():
        for z in range(depth):
            for half in range(2):
                dens[z + 1, half, pl.ds(height + ROWS, ROWS), :] = blank

    @pl.when(gy == 0)
    def _():
        halo[0] = blank

    @pl.when(gy == n_y - 1)
    def _():
        halo[1] = blank

    @pl.when(me == 0)
    def _():
        for half in range(2):
            dens[0, half, own_rows, :] = jnp.zeros((height, LANES), F32)

    @pl.when(me == n_z - 1)
    def _():
        for half in range(2):
            dens[depth + 1, half, own_rows, :] = jnp.zeros((height, LANES), F32)

    def tile(by):
        other = step(me, n_z, by)
        slot = by % n_z
        return pltpu.make_async_remote_copy(
            src_ref=send.at[other],
            dst_ref=recv.at[slot],
            send_sem=tile_send.at[slot],
            recv_sem=tile_recv.at[slot],
            device_id={"gz": other},
            device_id_type=MESH,
        )

    def colours(k, carry):
        away = lax.div(k + 1, 2)
        away = jnp.where(lax.rem(k, 2) == 1, away, blocks - away)
        block = lax.rem(lax.div(me, 2) + away, blocks)
        rows = pl.ds(pl.multiple_of(block * ROWS, ROWS), ROWS)
        base = block * ROWS
        here = pl.ds(pl.multiple_of(base + ROWS, ROWS), ROWS)
        sums = [[jnp.zeros((ROWS, LANES), F32) for _ in range(2)] for _ in range(3)]
        for z in range(depth):
            low, high = dens[z + 1, 0, here, :], dens[z + 1, 1, here, :]
            column = z * blocks + block
            west = pltpu.roll(halo[0], LANES - column, 1)
            east = pltpu.roll(halo[1], LANES - 1 - column, 1)
            low_up, high_up = pltpu.roll(low, 1, 1), pltpu.roll(high, 1, 1)
            low_down = pltpu.roll(low, LANES - 1, 1)
            high_down = pltpu.roll(high, LANES - 1, 1)
            slopes_y = (
                jnp.where(lane == LANES - 1, high_down, low_down)
                - jnp.where(lane == 0, west, low_up),
                jnp.where(lane == LANES - 1, east, high_down)
                - jnp.where(lane == 0, low_up, high_up),
            )
            for half in range(2):
                slope_z = dens[z + 2, half, here, :] - dens[z, half, here, :]
                slope_x = (
                    dens[z + 1, half, pl.ds(base + ROWS + 1, ROWS), :]
                    - dens[z + 1, half, pl.ds(base + ROWS - 1, ROWS), :]
                )
                slope_y = slopes_y[half]
                facing = jnp.abs(0.48 * slope_z + 0.36 * slope_x + 0.45 * slope_y)
                square = (
                    slope_z * slope_z + slope_x * slope_x + slope_y * slope_y + 4.0
                )
                shade = 0.25 + facing * lax.rsqrt(square)
                shaded = weight[z, half, rows, :] * shade
                bin_ = bins[z, half, rows, :]
                index, upper = bin_ & (LANES - 1), bin_ >= LANES
                for c in range(3):
                    sums[c][half] = sums[c][half] + shaded * looked(c, index, upper)
        for c in range(3):
            split(block, c, *sums[c])

        @pl.when(k == 2)
        def _():
            for by in (1, -1, 2, -2):
                tile(by).start()

        @pl.when(k == 4)
        def _():
            for by in (3, -3, 4, -4):
                tile(by).start()

        return carry

    lax.fori_loop(0, blocks, colours, 0)

    pl.semaphore_wait(known.at[2], 2)
    for by in (8, 7, -7, 6, -6, 5, -5):
        tile(by).start()

    recv[0] = send[me]
    for by in (1, -1, 2, -2, 3, -3, 4, -4, 5, -5, 6, -6, 7, -7, 8):
        tile(by).wait_recv()

    ahead = jnp.zeros((ROWS, LANES), F32)
    image = [jnp.zeros((ROWS, LANES), F32) for _ in range(3)]
    for rank in range(n_z):
        slot = inv[rank]
        through = jnp.exp2(ahead)
        for c in range(3):
            image[c] = image[c] + through * recv[slot, c]
        ahead = ahead + recv[slot, 3]
    image.append(1.0 - jnp.exp2(ahead))
    for c in range(4):
        out_ref[c, :, 0:LANES] = image[c][0:4, :]
        out_ref[c, :, LANES : 2 * LANES] = image[c][4:8, :]

    for copy in copies:
        copy.wait_send()
    for by in (1, -1, 2, -2, 3, -3, 4, -4, 5, -5, 6, -6, 7, -7, 8):
        tile(by).wait_send()


def local(density, bins, colour_table, opacity_table, order):
    depth, height, width = density.shape
    n_z = lax.axis_size("gz")
    scale = -3.0 / (depth * n_z) * math.log2(math.e)
    vmem = pl.BlockSpec(memory_space=pltpu.VMEM)
    anywhere = pl.BlockSpec(memory_space=pl.ANY)
    return pl.pallas_call(
        functools.partial(kernel, n_z, scale),
        out_shape=jax.ShapeDtypeStruct((4, height // n_z, width), F32),
        in_specs=[
            anywhere,
            anywhere,
            vmem,
            vmem,
            pl.BlockSpec(memory_space=pltpu.SMEM),
        ],
        out_specs=vmem,
        scratch_shapes=[
            pltpu.VMEM((depth + 2, 2, height + 2 * ROWS, LANES), F32),
            pltpu.VMEM((depth, 2, height, LANES), jnp.int32),
            pltpu.VMEM((4, 2, ROWS, LANES), F32),
            pltpu.VMEM((depth, 2, height, LANES), F32),
            pltpu.VMEM((2, ROWS, LANES), F32),
            pltpu.VMEM((2, ROWS, LANES), F32),
            pltpu.VMEM((n_z, 4, ROWS, LANES), F32),
            pltpu.VMEM((n_z, 4, ROWS, LANES), F32),
            pltpu.SMEM((n_z,), jnp.int32),
            pltpu.SemaphoreType.DMA((4,)),
            pltpu.SemaphoreType.DMA((6,)),
            pltpu.SemaphoreType.DMA((6,)),
            pltpu.SemaphoreType.DMA((n_z,)),
            pltpu.SemaphoreType.DMA((n_z,)),
            pltpu.SemaphoreType.REGULAR((3,)),
        ],
        compiler_params=pltpu.CompilerParams(collective_id=0, has_side_effects=True),
    )(density, bins, colour_table, opacity_table.reshape(1, -1), order)


def solution(mesh):
    return jax.shard_map(
        local,
        mesh=mesh,
        in_specs=(
            P("gz", "gx", "gy"),
            P("gz", "gx", "gy"),
            P(),
            P(),
            P("gx", "gy", None),
        ),
        out_specs=P(None, ("gx", "gz"), "gy"),
        check_vma=False,
    )
```

```python
import functools
import math

import jax
import jax.numpy as jnp
from jax import lax
from jax.experimental import pallas as pl
from jax.experimental.pallas import tpu as pltpu
from jax.sharding import PartitionSpec as P

MESH = pl.DeviceIdType.MESH
LANES = 128
ROWS = 8
F32 = jnp.float32


def kernel(
    n_z,
    scale,
    dens_hbm,
    bins_hbm,
    ctab_hbm,
    otab_hbm,
    order_hbm,
    out_ref,
    dens,
    bins,
    ctab_ref,
    otab_ref,
    order_ref,
    tabs,
    weight,
    edge,
    halo,
    send,
    recv,
    inv,
    load_sem,
    halo_send,
    halo_recv,
    depth_send,
    depth_recv,
    colour_send,
    colour_recv,
):
    gx, gy, me = lax.axis_index("gx"), lax.axis_index("gy"), lax.axis_index("gz")
    n_x, n_y = lax.axis_size("gx"), lax.axis_size("gy")
    depth, _, height, _ = bins.shape
    blocks = height // ROWS

    def step(index, count, by):
        return lax.rem(index + (by + count), count)

    neighbours = [
        {"gx": step(gx, n_x, -1)},
        {"gx": step(gx, n_x, 1)},
        {"gy": step(gy, n_y, -1)},
        {"gy": step(gy, n_y, 1)},
    ]
    below, above = {"gz": step(me, n_z, -1)}, {"gz": step(me, n_z, 1)}

    barrier = pltpu.get_barrier_semaphore()
    for other in neighbours:
        pl.semaphore_signal(barrier, inc=1, device_id=other, device_id_type=MESH)

    def greet(by, carry):
        pl.semaphore_signal(
            barrier,
            inc=1,
            device_id={"gz": lax.rem(me + by, n_z)},
            device_id_type=MESH,
        )
        return carry

    lax.fori_loop(1, n_z, greet, 0)

    loads = []
    for half in range(2):
        lanes = pl.ds(half * LANES, LANES)
        loads.append(
            pltpu.make_async_copy(
                dens_hbm.at[:, :, lanes],
                dens.at[pl.ds(1, depth), half, pl.ds(ROWS, height), :],
                load_sem.at[half],
            )
        )
    for half in range(2):
        lanes = pl.ds(half * LANES, LANES)
        loads.append(
            pltpu.make_async_copy(
                bins_hbm.at[:, :, lanes], bins.at[:, half], load_sem.at[2 + half]
            )
        )
    for index, (src, dst) in enumerate(
        ((ctab_hbm, ctab_ref), (otab_hbm, otab_ref), (order_hbm, order_ref))
    ):
        loads.append(pltpu.make_async_copy(src, dst, load_sem.at[4 + index]))
    for load in loads:
        load.start()
    loads[4].wait()
    loads[5].wait()

    table = jnp.concatenate(
        [ctab_ref[...].astype(F32), otab_ref[...].astype(F32).reshape(1, -1) * scale], axis=0
    )
    for c in range(4):
        for half in range(2):
            row = table[c : c + 1, half * LANES : (half + 1) * LANES]
            tabs[c, half] = jnp.broadcast_to(row, (ROWS, LANES))

    loads[0].wait()
    loads[1].wait()

    lane = lax.broadcasted_iota(jnp.int32, (ROWS, LANES), 1)
    sub = lax.broadcasted_iota(jnp.int32, (ROWS, LANES), 0)

    first = jnp.zeros((ROWS, LANES), F32)
    last = jnp.zeros((ROWS, LANES), F32)
    for z in range(depth):
        for b in range(blocks):
            k = z * blocks + b
            rows = pl.ds(ROWS + b * ROWS, ROWS)
            first = jnp.where(
                lane == k, jnp.broadcast_to(dens[z + 1, 0, rows, 0:1], first.shape), first
            )
            last = jnp.where(
                lane == k,
                jnp.broadcast_to(dens[z + 1, 1, rows, LANES - 1 : LANES], last.shape),
                last,
            )
    edge[0] = first
    edge[1] = last
    def split(block, channel, low, high):
        send[2 * block, channel] = jnp.where(sub < 4, low, pltpu.roll(high, 4, 0))
        send[2 * block + 1, channel] = jnp.where(sub < 4, pltpu.roll(low, 4, 0), high)

    def looked(c, index, upper):
        return jnp.where(
            upper,
            jnp.take_along_axis(tabs[c, 1], index, axis=1, mode="promise_in_bounds"),
            jnp.take_along_axis(tabs[c, 0], index, axis=1, mode="promise_in_bounds"),
        )

    loads[2].wait()
    loads[3].wait()

    def optical(block, carry):
        rows = pl.ds(pl.multiple_of(block * ROWS, ROWS), ROWS)
        padded = pl.ds(pl.multiple_of(block * ROWS + ROWS, ROWS), ROWS)
        ends = []
        for half in range(2):
            total = jnp.zeros((ROWS, LANES), F32)
            before = jnp.ones((ROWS, LANES), F32)
            for z in range(depth):
                bin_ = bins[z, half, rows, :]
                sigma = looked(3, bin_ & (LANES - 1), bin_ >= LANES)
                total = total + sigma * dens[z + 1, half, padded, :]
                after = jnp.exp2(total)
                weight[z, half, rows, :] = before - after
                before = after
            ends.append(total)
        split(block, 3, *ends)
        return carry

    lax.fori_loop(0, blocks, optical, 0)

    def depth_to(other):
        slot = lax.rem(other - me + n_z, n_z)
        return pltpu.make_async_remote_copy(
            src_ref=send.at[other, 3],
            dst_ref=recv.at[slot, 3],
            send_sem=depth_send.at[slot],
            recv_sem=depth_recv.at[slot],
            device_id={"gz": other},
            device_id_type=MESH,
        )

    def colour_to(other):
        slot = lax.rem(other - me + n_z, n_z)
        return pltpu.make_async_remote_copy(
            src_ref=send.at[other, pl.ds(0, 3)],
            dst_ref=recv.at[slot, pl.ds(0, 3)],
            send_sem=colour_send.at[slot],
            recv_sem=colour_recv.at[slot],
            device_id={"gz": other},
            device_id_type=MESH,
        )

    def remote(src, dst, index, other):
        return pltpu.make_async_remote_copy(
            src_ref=src,
            dst_ref=dst,
            send_sem=halo_send.at[index],
            recv_sem=halo_recv.at[index],
            device_id=other,
            device_id_type=MESH,
        )

    own_rows = pl.ds(ROWS, height)
    own_planes = pl.ds(1, depth)
    z_up = remote(
        dens.at[depth, :, own_rows, :], dens.at[0, :, own_rows, :], 0, above
    )
    z_down = remote(
        dens.at[1, :, own_rows, :],
        dens.at[depth + 1, :, own_rows, :],
        1,
        below,
    )
    x_up = remote(
        dens.at[own_planes, :, pl.ds(height, ROWS), :],
        dens.at[own_planes, :, pl.ds(0, ROWS), :],
        2,
        neighbours[1],
    )
    x_down = remote(
        dens.at[own_planes, :, pl.ds(ROWS, ROWS), :],
        dens.at[own_planes, :, pl.ds(height + ROWS, ROWS), :],
        3,
        neighbours[0],
    )

    y_up = remote(edge.at[1], halo.at[0], 4, neighbours[3])
    y_down = remote(edge.at[0], halo.at[1], 5, neighbours[2])
    pl.semaphore_wait(barrier, len(neighbours) + n_z - 1)
    copies = [z_up, z_down, y_up, y_down, x_up, x_down]
    for copy in copies:
        copy.start()

    def send_depth(by, carry):
        depth_to(lax.rem(me + by, n_z)).start()
        return carry

    lax.fori_loop(1, n_z, send_depth, 0)
    loads[6].wait()

    def place(rank, carry):
        slot = jnp.int32(0)
        for b in range(n_z):
            here = lax.rem(me + (n_z - b), n_z)
            slot = jnp.where(order_ref[0, 0, b] == rank, here, slot)
        inv[rank] = slot
        return carry

    lax.fori_loop(0, n_z, place, 0)

    for copy in copies:
        copy.wait_recv()

    blank = jnp.zeros((ROWS, LANES), F32)

    @pl.when(gx == 0)
    def _():
        for z in range(depth):
            for half in range(2):
                dens[z + 1, half, pl.ds(0, ROWS), :] = blank

    @pl.when(gx == n_x - 1)
    def _():
        for z in range(depth):
            for half in range(2):
                dens[z + 1, half, pl.ds(height + ROWS, ROWS), :] = blank

    @pl.when(gy == 0)
    def _():
        halo[0] = blank

    @pl.when(gy == n_y - 1)
    def _():
        halo[1] = blank

    @pl.when(me == 0)
    def _():
        for half in range(2):
            dens[0, half, own_rows, :] = jnp.zeros((height, LANES), F32)

    @pl.when(me == n_z - 1)
    def _():
        for half in range(2):
            dens[depth + 1, half, own_rows, :] = jnp.zeros((height, LANES), F32)

    def colours(k, carry):
        block = k
        rows = pl.ds(pl.multiple_of(block * ROWS, ROWS), ROWS)
        base = block * ROWS
        here = pl.ds(pl.multiple_of(base + ROWS, ROWS), ROWS)
        sums = [[jnp.zeros((ROWS, LANES), F32) for _ in range(2)] for _ in range(3)]
        for z in range(depth):
            low, high = dens[z + 1, 0, here, :], dens[z + 1, 1, here, :]
            column = z * blocks + block
            west = pltpu.roll(halo[0], LANES - column, 1)
            east = pltpu.roll(halo[1], LANES - 1 - column, 1)
            low_up, high_up = pltpu.roll(low, 1, 1), pltpu.roll(high, 1, 1)
            low_down = pltpu.roll(low, LANES - 1, 1)
            high_down = pltpu.roll(high, LANES - 1, 1)
            slopes_y = (
                jnp.where(lane == LANES - 1, high_down, low_down)
                - jnp.where(lane == 0, west, low_up),
                jnp.where(lane == LANES - 1, east, high_down)
                - jnp.where(lane == 0, low_up, high_up),
            )
            for half in range(2):
                slope_z = dens[z + 2, half, here, :] - dens[z, half, here, :]
                slope_x = (
                    dens[z + 1, half, pl.ds(base + ROWS + 1, ROWS), :]
                    - dens[z + 1, half, pl.ds(base + ROWS - 1, ROWS), :]
                )
                slope_y = slopes_y[half]
                facing = jnp.abs(0.48 * slope_z + 0.36 * slope_x + 0.45 * slope_y)
                square = (
                    slope_z * slope_z + slope_x * slope_x + slope_y * slope_y + 4.0
                )
                shade = 0.25 + facing * lax.rsqrt(square)
                shaded = weight[z, half, rows, :] * shade
                bin_ = bins[z, half, rows, :]
                index, upper = bin_ & (LANES - 1), bin_ >= LANES
                for c in range(3):
                    sums[c][half] = sums[c][half] + shaded * looked(c, index, upper)
        for c in range(3):
            split(block, c, *sums[c])

        for other in (2 * block, 2 * block + 1):

            @pl.when(other != me)
            def _():
                colour_to(other).start()

        return carry

    lax.fori_loop(0, blocks, colours, 0)

    recv[0] = send[me]

    def arrive(by, carry):
        other = lax.rem(me + by, n_z)
        depth_to(other).wait_recv()
        colour_to(other).wait_recv()
        return carry

    lax.fori_loop(1, n_z, arrive, 0)

    ahead = jnp.zeros((ROWS, LANES), F32)
    image = [jnp.zeros((ROWS, LANES), F32) for _ in range(3)]
    for rank in range(n_z):
        slot = inv[rank]
        through = jnp.exp2(ahead)
        for c in range(3):
            image[c] = image[c] + through * recv[slot, c]
        ahead = ahead + recv[slot, 3]
    image.append(1.0 - jnp.exp2(ahead))
    for c in range(4):
        out_ref[c, :, 0:LANES] = image[c][0:4, :]
        out_ref[c, :, LANES : 2 * LANES] = image[c][4:8, :]

    for copy in copies:
        copy.wait_send()

    def leave(by, carry):
        other = lax.rem(me + by, n_z)
        depth_to(other).wait_send()
        colour_to(other).wait_send()
        return carry

    lax.fori_loop(1, n_z, leave, 0)


def local(density, bins, colour_table, opacity_table, order):
    depth, height, width = density.shape
    n_z = lax.axis_size("gz")
    scale = -3.0 / (depth * n_z) * math.log2(math.e)
    vmem = pl.BlockSpec(memory_space=pltpu.VMEM)
    anywhere = pl.BlockSpec(memory_space=pl.ANY)
    return pl.pallas_call(
        functools.partial(kernel, n_z, scale),
        out_shape=jax.ShapeDtypeStruct((4, height // n_z, width), F32),
        in_specs=[anywhere] * 5,
        out_specs=vmem,
        scratch_shapes=[
            pltpu.VMEM((depth + 2, 2, height + 2 * ROWS, LANES), F32),
            pltpu.VMEM((depth, 2, height, LANES), jnp.int32),
            pltpu.VMEM(colour_table.shape, colour_table.dtype),
            pltpu.VMEM(opacity_table.shape, opacity_table.dtype),
            pltpu.SMEM(order.shape, order.dtype),
            pltpu.VMEM((4, 2, ROWS, LANES), F32),
            pltpu.VMEM((depth, 2, height, LANES), F32),
            pltpu.VMEM((2, ROWS, LANES), F32),
            pltpu.VMEM((2, ROWS, LANES), F32),
            pltpu.VMEM((n_z, 4, ROWS, LANES), F32),
            pltpu.VMEM((n_z, 4, ROWS, LANES), F32),
            pltpu.SMEM((n_z,), jnp.int32),
            pltpu.SemaphoreType.DMA((7,)),
            pltpu.SemaphoreType.DMA((6,)),
            pltpu.SemaphoreType.DMA((6,)),
            pltpu.SemaphoreType.DMA((n_z,)),
            pltpu.SemaphoreType.DMA((n_z,)),
            pltpu.SemaphoreType.DMA((n_z,)),
            pltpu.SemaphoreType.DMA((n_z,)),
        ],
        compiler_params=pltpu.CompilerParams(collective_id=0, has_side_effects=True),
    )(density, bins, colour_table, opacity_table, order)


def solution(mesh):
    return jax.shard_map(
        local,
        mesh=mesh,
        in_specs=(
            P("gz", "gx", "gy"),
            P("gz", "gx", "gy"),
            P(),
            P(),
            P("gx", "gy", None),
        ),
        out_specs=P(None, ("gx", "gz"), "gy"),
        check_vma=False,
    )
```

```python
import functools
import math

import jax
import jax.numpy as jnp
from jax import lax
from jax.experimental import pallas as pl
from jax.experimental.pallas import tpu as pltpu
from jax.sharding import PartitionSpec as P

MESH = pl.DeviceIdType.MESH
LANES = 128
ROWS = 8
PARTS = 4
F32 = jnp.float32


def kernel(
    n_z,
    scale,
    dens_hbm,
    bins_hbm,
    ctab_hbm,
    otab_hbm,
    order_hbm,
    out_ref,
    dens,
    bins,
    ctab_ref,
    otab_ref,
    order_ref,
    tabs,
    weight,
    edge,
    halo,
    rim,
    rim_halo,
    send,
    recv,
    inv,
    load_sem,
    halo_send,
    halo_recv,
    depth_send,
    depth_recv,
    colour_send,
    colour_recv,
    known,
):
    gx, gy, me = lax.axis_index("gx"), lax.axis_index("gy"), lax.axis_index("gz")
    n_x, n_y = lax.axis_size("gx"), lax.axis_size("gy")
    depth, _, height, _ = bins.shape
    blocks = height // ROWS

    def step(index, count, by):
        return lax.rem(index + (by + count), count)

    neighbours = [
        {"gx": step(gx, n_x, -1)},
        {"gx": step(gx, n_x, 1)},
        {"gy": step(gy, n_y, -1)},
        {"gy": step(gy, n_y, 1)},
    ]
    below, above = {"gz": step(me, n_z, -1)}, {"gz": step(me, n_z, 1)}

    reach = n_z // 4
    barrier = pltpu.get_barrier_semaphore()

    def greet(by, carry):
        for sign in (-1, 1):
            pl.semaphore_signal(
                barrier,
                inc=1,
                device_id={"gz": lax.rem(me + sign * (reach - by) + n_z, n_z)},
                device_id_type=MESH,
            )
        return carry

    lax.fori_loop(0, reach, greet, 0)
    for other in neighbours:
        pl.semaphore_signal(barrier, inc=1, device_id=other, device_id_type=MESH)

    loads = []
    for half in range(2):
        lanes = pl.ds(half * LANES, LANES)
        loads.append(
            pltpu.make_async_copy(
                dens_hbm.at[:, :, lanes],
                dens.at[pl.ds(1, depth), half, pl.ds(ROWS, height), :],
                load_sem.at[half],
            )
        )
    for half in range(2):
        lanes = pl.ds(half * LANES, LANES)
        loads.append(
            pltpu.make_async_copy(
                bins_hbm.at[:, :, lanes], bins.at[:, half], load_sem.at[2 + half]
            )
        )
    for index, (src, dst) in enumerate(
        ((ctab_hbm, ctab_ref), (otab_hbm, otab_ref), (order_hbm, order_ref))
    ):
        loads.append(pltpu.make_async_copy(src, dst, load_sem.at[4 + index]))
    for load in loads:
        load.start()
    loads[4].wait()
    loads[5].wait()

    table = jnp.concatenate(
        [ctab_ref[...].astype(F32), otab_ref[...].astype(F32).reshape(1, -1) * scale], axis=0
    )
    for c in range(4):
        for half in range(2):
            row = table[c : c + 1, half * LANES : (half + 1) * LANES]
            tabs[c, half] = jnp.broadcast_to(row, (ROWS, LANES))

    loads[0].wait()
    loads[1].wait()

    lane = lax.broadcasted_iota(jnp.int32, (ROWS, LANES), 1)
    sub = lax.broadcasted_iota(jnp.int32, (ROWS, LANES), 0)

    first = jnp.zeros((ROWS, LANES), F32)
    last = jnp.zeros((ROWS, LANES), F32)
    for z in range(depth):
        for b in range(blocks):
            k = z * blocks + b
            rows = pl.ds(ROWS + b * ROWS, ROWS)
            first = jnp.where(
                lane == k, jnp.broadcast_to(dens[z + 1, 0, rows, 0:1], first.shape), first
            )
            last = jnp.where(
                lane == k,
                jnp.broadcast_to(dens[z + 1, 1, rows, LANES - 1 : LANES], last.shape),
                last,
            )
    edge[0] = first
    edge[1] = last
    def split(block, channel, low, high):
        send[2 * block, channel] = jnp.where(sub < 4, low, pltpu.roll(high, 4, 0))
        send[2 * block + 1, channel] = jnp.where(sub < 4, pltpu.roll(low, 4, 0), high)

    def looked(c, index, upper):
        return jnp.where(
            upper,
            jnp.take_along_axis(tabs[c, 1], index, axis=1, mode="promise_in_bounds"),
            jnp.take_along_axis(tabs[c, 0], index, axis=1, mode="promise_in_bounds"),
        )

    loads[2].wait()
    loads[3].wait()

    def optical(block, carry):
        rows = pl.ds(pl.multiple_of(block * ROWS, ROWS), ROWS)
        padded = pl.ds(pl.multiple_of(block * ROWS + ROWS, ROWS), ROWS)
        ends = []
        for half in range(2):
            total = jnp.zeros((ROWS, LANES), F32)
            before = jnp.ones((ROWS, LANES), F32)
            for z in range(depth):
                bin_ = bins[z, half, rows, :]
                sigma = looked(3, bin_ & (LANES - 1), bin_ >= LANES)
                total = total + sigma * dens[z + 1, half, padded, :]
                after = jnp.exp2(total)
                weight[z, half, rows, :] = before - after
                before = after
            ends.append(total)
        split(block, 3, *ends)
        return carry

    lax.fori_loop(0, blocks, optical, 0)

    def depth_to(other):
        slot = lax.rem(other - me + n_z, n_z)
        return pltpu.make_async_remote_copy(
            src_ref=send.at[other, 3],
            dst_ref=recv.at[slot, 3],
            send_sem=depth_send.at[slot],
            recv_sem=depth_recv.at[slot],
            device_id={"gz": other},
            device_id_type=MESH,
        )

    def colour_to(other):
        slot = lax.rem(other - me + n_z, n_z)
        return pltpu.make_async_remote_copy(
            src_ref=send.at[other, pl.ds(0, 3)],
            dst_ref=recv.at[slot, pl.ds(0, 3)],
            send_sem=colour_send.at[slot],
            recv_sem=colour_recv.at[slot],
            device_id={"gz": other},
            device_id_type=MESH,
        )

    def remote(src, dst, index, other):
        return pltpu.make_async_remote_copy(
            src_ref=src,
            dst_ref=dst,
            send_sem=halo_send.at[index],
            recv_sem=halo_recv.at[index],
            device_id=other,
            device_id_type=MESH,
        )

    piece = height // PARTS

    def z_up(part):
        rows = pl.ds(pl.multiple_of(ROWS + part * piece, ROWS), piece)
        return remote(
            dens.at[depth, :, rows, :], dens.at[0, :, rows, :], 4 + part, above
        )

    def z_down(part):
        rows = pl.ds(pl.multiple_of(ROWS + part * piece, ROWS), piece)
        return remote(
            dens.at[1, :, rows, :],
            dens.at[depth + 1, :, rows, :],
            4 + PARTS + part,
            below,
        )

    for half in range(2):
        top = jnp.zeros((ROWS, LANES), F32)
        bottom = jnp.zeros((ROWS, LANES), F32)
        for z in range(depth):
            row = dens[z + 1, half, pl.ds(ROWS, 1), :]
            top = jnp.where(sub == z, jnp.broadcast_to(row, top.shape), top)
            row = dens[z + 1, half, pl.ds(height + ROWS - 1, 1), :]
            bottom = jnp.where(sub == z, jnp.broadcast_to(row, top.shape), bottom)
        rim[0, half] = top
        rim[1, half] = bottom
    x_up = remote(rim.at[1], rim_halo.at[0], 2, neighbours[1])
    x_down = remote(rim.at[0], rim_halo.at[1], 3, neighbours[0])

    @pl.when(me == 0)
    def _():
        for half in range(2):
            dens[0, half, pl.ds(ROWS, height), :] = jnp.zeros((height, LANES), F32)

    @pl.when(me == n_z - 1)
    def _():
        for half in range(2):
            dens[depth + 1, half, pl.ds(ROWS, height), :] = jnp.zeros(
                (height, LANES), F32
            )

    y_up = remote(edge.at[1], halo.at[0], 0, neighbours[3])
    y_down = remote(edge.at[0], halo.at[1], 1, neighbours[2])
    pl.semaphore_wait(barrier, len(neighbours) + 2 * reach)
    copies = [y_up, y_down, x_up, x_down]
    for copy in copies:
        copy.start()

    @pl.when(me != n_z - 1)
    def _():
        for part in range(PARTS):
            z_up(part).start()

    @pl.when(me != 0)
    def _():
        for part in range(PARTS):
            z_down(part).start()

    for sign in (-1, 1):
        pl.semaphore_signal(
            known,
            inc=1,
            device_id={"gz": step(me, n_z, sign * reach)},
            device_id_type=MESH,
        )

    def send_depth(by, carry):
        for sign in (-1, 1):
            depth_to(lax.rem(me + sign * by + n_z, n_z)).start()
        return carry

    lax.fori_loop(1, reach + 1, send_depth, 0)
    pl.semaphore_wait(known, 2)
    lax.fori_loop(reach + 1, n_z // 2, send_depth, 0)
    depth_to(lax.rem(me + n_z // 2, n_z)).start()

    for copy in copies:
        copy.wait_recv()

    blank = jnp.zeros((ROWS, LANES), F32)

    @pl.when(gx == 0)
    def _():
        for half in range(2):
            rim_halo[0, half] = blank

    @pl.when(gx == n_x - 1)
    def _():
        for half in range(2):
            rim_halo[1, half] = blank

    @pl.when(gy == 0)
    def _():
        halo[0] = blank

    @pl.when(gy == n_y - 1)
    def _():
        halo[1] = blank

    for half in range(2):
        before, after = rim_halo[0, half], rim_halo[1, half]
        for z in range(depth):
            dens[z + 1, half, pl.ds(ROWS - 1, 1), :] = before[z : z + 1, :]
            dens[z + 1, half, pl.ds(height + ROWS, 1), :] = after[z : z + 1, :]

    def colours(block, carry):
        part = lax.div(block * PARTS, blocks)

        @pl.when(lax.rem(block * PARTS, blocks) == 0)
        def _():
            @pl.when(me != 0)
            def _():
                z_up(part).wait_recv()

            @pl.when(me != n_z - 1)
            def _():
                z_down(part).wait_recv()

        rows = pl.ds(pl.multiple_of(block * ROWS, ROWS), ROWS)
        base = block * ROWS
        here = pl.ds(pl.multiple_of(base + ROWS, ROWS), ROWS)
        sums = [[jnp.zeros((ROWS, LANES), F32) for _ in range(2)] for _ in range(3)]
        for z in range(depth):
            low, high = dens[z + 1, 0, here, :], dens[z + 1, 1, here, :]
            column = z * blocks + block
            west = pltpu.roll(halo[0], LANES - column, 1)
            east = pltpu.roll(halo[1], LANES - 1 - column, 1)
            low_up, high_up = pltpu.roll(low, 1, 1), pltpu.roll(high, 1, 1)
            low_down = pltpu.roll(low, LANES - 1, 1)
            high_down = pltpu.roll(high, LANES - 1, 1)
            slopes_y = (
                jnp.where(lane == LANES - 1, high_down, low_down)
                - jnp.where(lane == 0, west, low_up),
                jnp.where(lane == LANES - 1, east, high_down)
                - jnp.where(lane == 0, low_up, high_up),
            )
            for half in range(2):
                slope_z = dens[z + 2, half, here, :] - dens[z, half, here, :]
                slope_x = (
                    dens[z + 1, half, pl.ds(base + ROWS + 1, ROWS), :]
                    - dens[z + 1, half, pl.ds(base + ROWS - 1, ROWS), :]
                )
                slope_y = slopes_y[half]
                facing = jnp.abs(0.48 * slope_z + 0.36 * slope_x + 0.45 * slope_y)
                square = (
                    slope_z * slope_z + slope_x * slope_x + slope_y * slope_y + 4.0
                )
                shade = 0.25 + facing * lax.rsqrt(square)
                shaded = weight[z, half, rows, :] * shade
                bin_ = bins[z, half, rows, :]
                index, upper = bin_ & (LANES - 1), bin_ >= LANES
                for c in range(3):
                    sums[c][half] = sums[c][half] + shaded * looked(c, index, upper)
        for c in range(3):
            split(block, c, *sums[c])

        for other in (2 * block, 2 * block + 1):

            @pl.when(other != me)
            def _():
                colour_to(other).start()

        return carry

    lax.fori_loop(0, blocks, colours, 0)

    loads[6].wait()

    def place(rank, carry):
        slot = jnp.int32(0)
        for b in range(n_z):
            here = lax.rem(me + (n_z - b), n_z)
            slot = jnp.where(order_ref[0, 0, b] == rank, here, slot)
        inv[rank] = slot
        return carry

    lax.fori_loop(0, n_z, place, 0)

    recv[0] = send[me]

    def arrive(by, carry):
        other = lax.rem(me + by, n_z)
        depth_to(other).wait_recv()
        colour_to(other).wait_recv()
        return carry

    lax.fori_loop(1, n_z, arrive, 0)

    ahead = jnp.zeros((ROWS, LANES), F32)
    image = [jnp.zeros((ROWS, LANES), F32) for _ in range(3)]
    for rank in range(n_z):
        slot = inv[rank]
        through = jnp.exp2(ahead)
        for c in range(3):
            image[c] = image[c] + through * recv[slot, c]
        ahead = ahead + recv[slot, 3]
    image.append(1.0 - jnp.exp2(ahead))
    for c in range(4):
        out_ref[c, :, 0:LANES] = image[c][0:4, :]
        out_ref[c, :, LANES : 2 * LANES] = image[c][4:8, :]

    for copy in copies:
        copy.wait_send()

    @pl.when(me != n_z - 1)
    def _():
        for part in range(PARTS):
            z_up(part).wait_send()

    @pl.when(me != 0)
    def _():
        for part in range(PARTS):
            z_down(part).wait_send()


    def leave(by, carry):
        other = lax.rem(me + by, n_z)
        depth_to(other).wait_send()
        colour_to(other).wait_send()
        return carry

    lax.fori_loop(1, n_z, leave, 0)


def local(density, bins, colour_table, opacity_table, order):
    depth, height, width = density.shape
    n_z = lax.axis_size("gz")
    scale = -3.0 / (depth * n_z) * math.log2(math.e)
    vmem = pl.BlockSpec(memory_space=pltpu.VMEM)
    anywhere = pl.BlockSpec(memory_space=pl.ANY)
    return pl.pallas_call(
        functools.partial(kernel, n_z, scale),
        out_shape=pltpu.VMEM((4, height // n_z, width), F32),
        in_specs=[anywhere] * 5,
        out_specs=vmem,
        scratch_shapes=[
            pltpu.VMEM((depth + 2, 2, height + 2 * ROWS, LANES), F32),
            pltpu.VMEM((depth, 2, height, LANES), jnp.int32),
            pltpu.VMEM(colour_table.shape, colour_table.dtype),
            pltpu.VMEM(opacity_table.shape, opacity_table.dtype),
            pltpu.SMEM(order.shape, order.dtype),
            pltpu.VMEM((4, 2, ROWS, LANES), F32),
            pltpu.VMEM((depth, 2, height, LANES), F32),
            pltpu.VMEM((2, ROWS, LANES), F32),
            pltpu.VMEM((2, ROWS, LANES), F32),
            pltpu.VMEM((2, 2, ROWS, LANES), F32),
            pltpu.VMEM((2, 2, ROWS, LANES), F32),
            pltpu.VMEM((n_z, 4, ROWS, LANES), F32),
            pltpu.VMEM((n_z, 4, ROWS, LANES), F32),
            pltpu.SMEM((n_z,), jnp.int32),
            pltpu.SemaphoreType.DMA((7,)),
            pltpu.SemaphoreType.DMA((4 + 2 * PARTS,)),
            pltpu.SemaphoreType.DMA((4 + 2 * PARTS,)),
            pltpu.SemaphoreType.DMA((n_z,)),
            pltpu.SemaphoreType.DMA((n_z,)),
            pltpu.SemaphoreType.DMA((n_z,)),
            pltpu.SemaphoreType.DMA((n_z,)),
            pltpu.SemaphoreType.REGULAR,
        ],
        compiler_params=pltpu.CompilerParams(collective_id=0, has_side_effects=True),
    )(density, bins, colour_table, opacity_table, order)


def solution(mesh):
    return jax.shard_map(
        local,
        mesh=mesh,
        in_specs=(
            P("gz", "gx", "gy"),
            P("gz", "gx", "gy"),
            P(),
            P(),
            P("gx", "gy", None),
        ),
        out_specs=P(None, ("gx", "gz"), "gy"),
        check_vma=False,
    )
```

```python
import functools
import math

import jax
import jax.numpy as jnp
from jax import lax
from jax.experimental import pallas as pl
from jax.experimental.pallas import tpu as pltpu
from jax.sharding import PartitionSpec as P

MESH = pl.DeviceIdType.MESH
LANES = 128
ROWS = 8
F32 = jnp.float32


def kernel(
    n_z,
    scale,
    dens_hbm,
    bins_hbm,
    ctab_hbm,
    otab_hbm,
    order_hbm,
    out_ref,
    dens,
    bins,
    ctab_ref,
    otab_ref,
    order_ref,
    tabs,
    weight,
    edge,
    halo,
    rim,
    rim_halo,
    send,
    recv,
    inv,
    load_sem,
    halo_send,
    halo_recv,
    depth_send,
    depth_recv,
    colour_send,
    colour_recv,
    known,
):
    gx, gy, me = lax.axis_index("gx"), lax.axis_index("gy"), lax.axis_index("gz")
    n_x, n_y = lax.axis_size("gx"), lax.axis_size("gy")
    depth, _, height, _ = bins.shape
    blocks = height // ROWS

    def step(index, count, by):
        return lax.rem(index + (by + count), count)

    neighbours = [
        {"gx": step(gx, n_x, -1)},
        {"gx": step(gx, n_x, 1)},
        {"gy": step(gy, n_y, -1)},
        {"gy": step(gy, n_y, 1)},
    ]
    below, above = {"gz": step(me, n_z, -1)}, {"gz": step(me, n_z, 1)}

    reach = n_z // 4
    barrier = pltpu.get_barrier_semaphore()

    def greet(by, carry):
        for sign in (-1, 1):
            pl.semaphore_signal(
                barrier,
                inc=1,
                device_id={"gz": lax.rem(me + sign * (reach - by) + n_z, n_z)},
                device_id_type=MESH,
            )
        return carry

    lax.fori_loop(0, reach, greet, 0)
    for other in neighbours:
        pl.semaphore_signal(barrier, inc=1, device_id=other, device_id_type=MESH)

    loads = []
    for half in range(2):
        lanes = pl.ds(half * LANES, LANES)
        loads.append(
            pltpu.make_async_copy(
                dens_hbm.at[:, :, lanes],
                dens.at[pl.ds(1, depth), half, pl.ds(ROWS, height), :],
                load_sem.at[half],
            )
        )
    for half in range(2):
        lanes = pl.ds(half * LANES, LANES)
        loads.append(
            pltpu.make_async_copy(
                bins_hbm.at[:, :, lanes], bins.at[:, half], load_sem.at[2 + half]
            )
        )
    for index, (src, dst) in enumerate(
        ((ctab_hbm, ctab_ref), (otab_hbm, otab_ref), (order_hbm, order_ref))
    ):
        loads.append(pltpu.make_async_copy(src, dst, load_sem.at[4 + index]))
    for load in loads:
        load.start()
    loads[4].wait()
    loads[5].wait()

    table = jnp.concatenate(
        [ctab_ref[...].astype(F32), otab_ref[...].astype(F32).reshape(1, -1) * scale], axis=0
    )
    for c in range(4):
        for half in range(2):
            row = table[c : c + 1, half * LANES : (half + 1) * LANES]
            tabs[c, half] = jnp.broadcast_to(row, (ROWS, LANES))

    loads[0].wait()
    loads[1].wait()

    lane = lax.broadcasted_iota(jnp.int32, (ROWS, LANES), 1)
    sub = lax.broadcasted_iota(jnp.int32, (ROWS, LANES), 0)

    first = jnp.zeros((ROWS, LANES), F32)
    last = jnp.zeros((ROWS, LANES), F32)
    for z in range(depth):
        for b in range(blocks):
            k = z * blocks + b
            rows = pl.ds(ROWS + b * ROWS, ROWS)
            first = jnp.where(
                lane == k, jnp.broadcast_to(dens[z + 1, 0, rows, 0:1], first.shape), first
            )
            last = jnp.where(
                lane == k,
                jnp.broadcast_to(dens[z + 1, 1, rows, LANES - 1 : LANES], last.shape),
                last,
            )
    edge[0] = first
    edge[1] = last
    def split(block, channel, low, high):
        send[2 * block, channel] = jnp.where(sub < 4, low, pltpu.roll(high, 4, 0))
        send[2 * block + 1, channel] = jnp.where(sub < 4, pltpu.roll(low, 4, 0), high)

    def looked(c, index, upper):
        return jnp.where(
            upper,
            jnp.take_along_axis(tabs[c, 1], index, axis=1, mode="promise_in_bounds"),
            jnp.take_along_axis(tabs[c, 0], index, axis=1, mode="promise_in_bounds"),
        )

    loads[2].wait()
    loads[3].wait()

    def optical(block, carry):
        rows = pl.ds(pl.multiple_of(block * ROWS, ROWS), ROWS)
        padded = pl.ds(pl.multiple_of(block * ROWS + ROWS, ROWS), ROWS)
        ends = []
        for half in range(2):
            total = jnp.zeros((ROWS, LANES), F32)
            before = jnp.ones((ROWS, LANES), F32)
            for z in range(depth):
                bin_ = bins[z, half, rows, :]
                sigma = looked(3, bin_ & (LANES - 1), bin_ >= LANES)
                total = total + sigma * dens[z + 1, half, padded, :]
                after = jnp.exp2(total)
                weight[z, half, rows, :] = before - after
                before = after
            ends.append(total)
        split(block, 3, *ends)
        return carry

    lax.fori_loop(0, blocks, optical, 0)

    def depth_to(other):
        slot = lax.rem(other - me + n_z, n_z)
        return pltpu.make_async_remote_copy(
            src_ref=send.at[other, 3],
            dst_ref=recv.at[slot, 3],
            send_sem=depth_send,
            recv_sem=depth_recv,
            device_id={"gz": other},
            device_id_type=MESH,
        )

    def colour_to(other):
        slot = lax.rem(other - me + n_z, n_z)
        return pltpu.make_async_remote_copy(
            src_ref=send.at[other, pl.ds(0, 3)],
            dst_ref=recv.at[slot, pl.ds(0, 3)],
            send_sem=colour_send,
            recv_sem=colour_recv,
            device_id={"gz": other},
            device_id_type=MESH,
        )

    def remote(src, dst, index, other):
        return pltpu.make_async_remote_copy(
            src_ref=src,
            dst_ref=dst,
            send_sem=halo_send.at[index],
            recv_sem=halo_recv.at[index],
            device_id=other,
            device_id_type=MESH,
        )

    rows = pl.ds(ROWS, height)
    z_up = remote(dens.at[depth, :, rows, :], dens.at[0, :, rows, :], 4, above)
    z_down = remote(dens.at[1, :, rows, :], dens.at[depth + 1, :, rows, :], 5, below)

    for half in range(2):
        top = jnp.zeros((ROWS, LANES), F32)
        bottom = jnp.zeros((ROWS, LANES), F32)
        for z in range(depth):
            row = dens[z + 1, half, pl.ds(ROWS, 1), :]
            top = jnp.where(sub == z, jnp.broadcast_to(row, top.shape), top)
            row = dens[z + 1, half, pl.ds(height + ROWS - 1, 1), :]
            bottom = jnp.where(sub == z, jnp.broadcast_to(row, top.shape), bottom)
        rim[0, half] = top
        rim[1, half] = bottom
    x_up = remote(rim.at[1], rim_halo.at[0], 2, neighbours[1])
    x_down = remote(rim.at[0], rim_halo.at[1], 3, neighbours[0])

    @pl.when(me == 0)
    def _():
        for half in range(2):
            dens[0, half, pl.ds(ROWS, height), :] = jnp.zeros((height, LANES), F32)

    @pl.when(me == n_z - 1)
    def _():
        for half in range(2):
            dens[depth + 1, half, pl.ds(ROWS, height), :] = jnp.zeros(
                (height, LANES), F32
            )

    y_up = remote(edge.at[1], halo.at[0], 0, neighbours[3])
    y_down = remote(edge.at[0], halo.at[1], 1, neighbours[2])
    pl.semaphore_wait(barrier, len(neighbours) + 2 * reach)
    has_before = (gy > 0, gx > 0, me > 0)
    has_after = (gy < n_y - 1, gx < n_x - 1, me < n_z - 1)
    upward, downward = (y_up, x_up, z_up), (y_down, x_down, z_down)

    def sides(act, towards):
        for copies, there in zip((upward, downward), towards):
            for copy, here in zip(copies, there):
                pl.when(here)(functools.partial(act, copy))

    sides(lambda copy: copy.start(), (has_after, has_before))

    for sign in (-1, 1):
        pl.semaphore_signal(
            known,
            inc=1,
            device_id={"gz": step(me, n_z, sign * reach)},
            device_id_type=MESH,
        )

    def send_depth(by, carry):
        for sign in (-1, 1):
            depth_to(lax.rem(me + sign * by + n_z, n_z)).start()
        return carry

    lax.fori_loop(1, reach + 1, send_depth, 0)
    pl.semaphore_wait(known, 2)
    lax.fori_loop(reach + 1, n_z // 2, send_depth, 0)
    depth_to(lax.rem(me + n_z // 2, n_z)).start()

    sides(lambda copy: copy.wait_recv(), (has_before, has_after))

    blank = jnp.zeros((ROWS, LANES), F32)

    @pl.when(gx == 0)
    def _():
        for half in range(2):
            rim_halo[0, half] = blank

    @pl.when(gx == n_x - 1)
    def _():
        for half in range(2):
            rim_halo[1, half] = blank

    @pl.when(gy == 0)
    def _():
        halo[0] = blank

    @pl.when(gy == n_y - 1)
    def _():
        halo[1] = blank

    for half in range(2):
        before, after = rim_halo[0, half], rim_halo[1, half]
        for z in range(depth):
            dens[z + 1, half, pl.ds(ROWS - 1, 1), :] = before[z : z + 1, :]
            dens[z + 1, half, pl.ds(height + ROWS, 1), :] = after[z : z + 1, :]

    def colours(k, carry):
        block = jnp.where(me < n_z // 2, jnp.where(k < 2, k, jnp.where(k < 6, k + 2, k - 4)), k)
        rows = pl.ds(pl.multiple_of(block * ROWS, ROWS), ROWS)
        base = block * ROWS
        here = pl.ds(pl.multiple_of(base + ROWS, ROWS), ROWS)
        sums = [[jnp.zeros((ROWS, LANES), F32) for _ in range(2)] for _ in range(3)]
        for z in range(depth):
            low, high = dens[z + 1, 0, here, :], dens[z + 1, 1, here, :]
            column = z * blocks + block
            west = pltpu.roll(halo[0], LANES - column, 1)
            east = pltpu.roll(halo[1], LANES - 1 - column, 1)
            low_up, high_up = pltpu.roll(low, 1, 1), pltpu.roll(high, 1, 1)
            low_down = pltpu.roll(low, LANES - 1, 1)
            high_down = pltpu.roll(high, LANES - 1, 1)
            slopes_y = (
                jnp.where(lane == LANES - 1, high_down, low_down)
                - jnp.where(lane == 0, west, low_up),
                jnp.where(lane == LANES - 1, east, high_down)
                - jnp.where(lane == 0, low_up, high_up),
            )
            for half in range(2):
                slope_z = dens[z + 2, half, here, :] - dens[z, half, here, :]
                slope_x = (
                    dens[z + 1, half, pl.ds(base + ROWS + 1, ROWS), :]
                    - dens[z + 1, half, pl.ds(base + ROWS - 1, ROWS), :]
                )
                slope_y = slopes_y[half]
                facing = jnp.abs(0.48 * slope_z + 0.36 * slope_x + 0.45 * slope_y)
                square = (
                    slope_z * slope_z + slope_x * slope_x + slope_y * slope_y + 4.0
                )
                shade = 0.25 + facing * lax.rsqrt(square)
                shaded = weight[z, half, rows, :] * shade
                bin_ = bins[z, half, rows, :]
                index, upper = bin_ & (LANES - 1), bin_ >= LANES
                for c in range(3):
                    sums[c][half] = sums[c][half] + shaded * looked(c, index, upper)
        for c in range(3):
            split(block, c, *sums[c])

        for other in (2 * block, 2 * block + 1):

            @pl.when(other != me)
            def _():
                colour_to(other).start()

        return carry

    lax.fori_loop(0, blocks, colours, 0)

    loads[6].wait()

    def place(rank, carry):
        slot = jnp.int32(0)
        for b in range(n_z):
            here = lax.rem(me + (n_z - b), n_z)
            slot = jnp.where(order_ref[0, 0, b] == rank, here, slot)
        inv[rank] = slot
        return carry

    lax.fori_loop(0, n_z, place, 0)

    recv[0] = send[me]

    others = pl.ds(1, n_z - 1)

    def all_tiles(channels, send_sem, recv_sem):
        return pltpu.make_async_remote_copy(
            src_ref=send.at[others, channels],
            dst_ref=recv.at[others, channels],
            send_sem=send_sem,
            recv_sem=recv_sem,
            device_id=above,
            device_id_type=MESH,
        )

    all_depths = all_tiles(3, depth_send, depth_recv)
    all_colours = all_tiles(pl.ds(0, 3), colour_send, colour_recv)
    all_depths.wait_recv()
    all_colours.wait_recv()

    ahead = jnp.zeros((ROWS, LANES), F32)
    image = [jnp.zeros((ROWS, LANES), F32) for _ in range(3)]
    for rank in range(n_z):
        slot = inv[rank]
        through = jnp.exp2(ahead)
        for c in range(3):
            image[c] = image[c] + through * recv[slot, c]
        ahead = ahead + recv[slot, 3]
    image.append(1.0 - jnp.exp2(ahead))
    for c in range(4):
        out_ref[c, :, 0:LANES] = image[c][0:4, :]
        out_ref[c, :, LANES : 2 * LANES] = image[c][4:8, :]

    sides(lambda copy: copy.wait_send(), (has_after, has_before))

    all_depths.wait_send()
    all_colours.wait_send()


def local(density, bins, colour_table, opacity_table, order):
    depth, height, width = density.shape
    n_z = lax.axis_size("gz")
    scale = -3.0 / (depth * n_z) * math.log2(math.e)
    vmem = pl.BlockSpec(memory_space=pltpu.VMEM)
    anywhere = pl.BlockSpec(memory_space=pl.ANY)
    return pl.pallas_call(
        functools.partial(kernel, n_z, scale),
        out_shape=pltpu.VMEM((4, height // n_z, width), F32),
        in_specs=[anywhere] * 5,
        out_specs=vmem,
        scratch_shapes=[
            pltpu.VMEM((depth + 2, 2, height + 2 * ROWS, LANES), F32),
            pltpu.VMEM((depth, 2, height, LANES), jnp.int32),
            pltpu.VMEM(colour_table.shape, colour_table.dtype),
            pltpu.VMEM(opacity_table.shape, opacity_table.dtype),
            pltpu.SMEM(order.shape, order.dtype),
            pltpu.VMEM((4, 2, ROWS, LANES), F32),
            pltpu.VMEM((depth, 2, height, LANES), F32),
            pltpu.VMEM((2, ROWS, LANES), F32),
            pltpu.VMEM((2, ROWS, LANES), F32),
            pltpu.VMEM((2, 2, ROWS, LANES), F32),
            pltpu.VMEM((2, 2, ROWS, LANES), F32),
            pltpu.VMEM((n_z, 4, ROWS, LANES), F32),
            pltpu.VMEM((n_z, 4, ROWS, LANES), F32),
            pltpu.SMEM((n_z,), jnp.int32),
            pltpu.SemaphoreType.DMA((7,)),
            pltpu.SemaphoreType.DMA((6,)),
            pltpu.SemaphoreType.DMA((6,)),
            pltpu.SemaphoreType.DMA,
            pltpu.SemaphoreType.DMA,
            pltpu.SemaphoreType.DMA,
            pltpu.SemaphoreType.DMA,
            pltpu.SemaphoreType.REGULAR,
        ],
        compiler_params=pltpu.CompilerParams(collective_id=0, has_side_effects=True),
    )(density, bins, colour_table, opacity_table, order)


def solution(mesh):
    return jax.shard_map(
        local,
        mesh=mesh,
        in_specs=(
            P("gz", "gx", "gy"),
            P("gz", "gx", "gy"),
            P(),
            P(),
            P("gx", "gy", None),
        ),
        out_specs=P(None, ("gx", "gz"), "gy"),
        check_vma=False,
    )
```

```python
import functools
import math

import jax
import jax.numpy as jnp
from jax import lax
from jax.experimental import pallas as pl
from jax.experimental.pallas import tpu as pltpu
from jax.sharding import PartitionSpec as P

MESH = pl.DeviceIdType.MESH
LANES = 128
ROWS = 8
F32 = jnp.float32


def kernel(
    n_z,
    scale,
    dens_hbm,
    bins_hbm,
    ctab_hbm,
    otab_hbm,
    order_hbm,
    out_ref,
    dens,
    bins,
    ctab_ref,
    otab_ref,
    order_ref,
    tabs,
    weight,
    tinted,
    edge,
    halo,
    rim,
    rim_halo,
    send,
    recv,
    inv,
    load_sem,
    halo_send,
    halo_recv,
    depth_send,
    depth_recv,
    colour_send,
    colour_recv,
    known,
):
    gx, gy, me = lax.axis_index("gx"), lax.axis_index("gy"), lax.axis_index("gz")
    n_x, n_y = lax.axis_size("gx"), lax.axis_size("gy")
    depth, _, height, _ = bins.shape
    blocks = height // ROWS

    def step(index, count, by):
        return lax.rem(index + (by + count), count)

    neighbours = [
        {"gx": step(gx, n_x, -1)},
        {"gx": step(gx, n_x, 1)},
        {"gy": step(gy, n_y, -1)},
        {"gy": step(gy, n_y, 1)},
    ]
    below, above = {"gz": step(me, n_z, -1)}, {"gz": step(me, n_z, 1)}

    reach = n_z // 4
    barrier = pltpu.get_barrier_semaphore()

    def greet(by, carry):
        for sign in (-1, 1):
            pl.semaphore_signal(
                barrier,
                inc=1,
                device_id={"gz": lax.rem(me + sign * (reach - by) + n_z, n_z)},
                device_id_type=MESH,
            )
        return carry

    lax.fori_loop(0, reach, greet, 0)
    for other in neighbours:
        pl.semaphore_signal(barrier, inc=1, device_id=other, device_id_type=MESH)

    loads = []
    for half in range(2):
        lanes = pl.ds(half * LANES, LANES)
        loads.append(
            pltpu.make_async_copy(
                dens_hbm.at[:, :, lanes],
                dens.at[pl.ds(1, depth), half, pl.ds(ROWS, height), :],
                load_sem.at[half],
            )
        )
    for half in range(2):
        lanes = pl.ds(half * LANES, LANES)
        loads.append(
            pltpu.make_async_copy(
                bins_hbm.at[:, :, lanes], bins.at[:, half], load_sem.at[2 + half]
            )
        )
    for index, (src, dst) in enumerate(
        ((ctab_hbm, ctab_ref), (otab_hbm, otab_ref), (order_hbm, order_ref))
    ):
        loads.append(pltpu.make_async_copy(src, dst, load_sem.at[4 + index]))
    for load in loads:
        load.start()
    loads[4].wait()
    loads[5].wait()

    table = jnp.concatenate(
        [ctab_ref[...].astype(F32), otab_ref[...].astype(F32).reshape(1, -1) * scale], axis=0
    )
    for c in range(4):
        for half in range(2):
            row = table[c : c + 1, half * LANES : (half + 1) * LANES]
            tabs[c, half] = jnp.broadcast_to(row, (ROWS, LANES))

    loads[0].wait()
    loads[1].wait()

    lane = lax.broadcasted_iota(jnp.int32, (ROWS, LANES), 1)
    sub = lax.broadcasted_iota(jnp.int32, (ROWS, LANES), 0)

    first = jnp.zeros((ROWS, LANES), F32)
    last = jnp.zeros((ROWS, LANES), F32)
    for z in range(depth):
        for b in range(blocks):
            k = z * blocks + b
            rows = pl.ds(ROWS + b * ROWS, ROWS)
            first = jnp.where(
                lane == k, jnp.broadcast_to(dens[z + 1, 0, rows, 0:1], first.shape), first
            )
            last = jnp.where(
                lane == k,
                jnp.broadcast_to(dens[z + 1, 1, rows, LANES - 1 : LANES], last.shape),
                last,
            )
    edge[0] = first
    edge[1] = last
    def split(block, channel, low, high):
        send[2 * block, channel] = jnp.where(sub < 4, low, pltpu.roll(high, 4, 0))
        send[2 * block + 1, channel] = jnp.where(sub < 4, pltpu.roll(low, 4, 0), high)

    def looked(c, index, upper):
        return jnp.where(
            upper,
            jnp.take_along_axis(tabs[c, 1], index, axis=1, mode="promise_in_bounds"),
            jnp.take_along_axis(tabs[c, 0], index, axis=1, mode="promise_in_bounds"),
        )

    loads[2].wait()
    loads[3].wait()

    def optical(block, carry):
        rows = pl.ds(pl.multiple_of(block * ROWS, ROWS), ROWS)
        padded = pl.ds(pl.multiple_of(block * ROWS + ROWS, ROWS), ROWS)
        ends = []
        for half in range(2):
            total = jnp.zeros((ROWS, LANES), F32)
            before = jnp.ones((ROWS, LANES), F32)
            for z in range(depth):
                bin_ = bins[z, half, rows, :]
                sigma = looked(3, bin_ & (LANES - 1), bin_ >= LANES)
                total = total + sigma * dens[z + 1, half, padded, :]
                after = jnp.exp2(total)
                weight[z, half, rows, :] = before - after
                before = after
            ends.append(total)
        split(block, 3, *ends)
        return carry

    lax.fori_loop(0, blocks, optical, 0)

    def depth_to(other):
        slot = lax.rem(other - me + n_z, n_z)
        return pltpu.make_async_remote_copy(
            src_ref=send.at[other, 3],
            dst_ref=recv.at[slot, 3],
            send_sem=depth_send,
            recv_sem=depth_recv,
            device_id={"gz": other},
            device_id_type=MESH,
        )

    def colour_to(other):
        slot = lax.rem(other - me + n_z, n_z)
        return pltpu.make_async_remote_copy(
            src_ref=send.at[other, pl.ds(0, 3)],
            dst_ref=recv.at[slot, pl.ds(0, 3)],
            send_sem=colour_send,
            recv_sem=colour_recv,
            device_id={"gz": other},
            device_id_type=MESH,
        )

    def remote(src, dst, index, other):
        return pltpu.make_async_remote_copy(
            src_ref=src,
            dst_ref=dst,
            send_sem=halo_send.at[index],
            recv_sem=halo_recv.at[index],
            device_id=other,
            device_id_type=MESH,
        )

    rows = pl.ds(ROWS, height)
    z_up = remote(dens.at[depth, :, rows, :], dens.at[0, :, rows, :], 4, above)
    z_down = remote(dens.at[1, :, rows, :], dens.at[depth + 1, :, rows, :], 5, below)

    for half in range(2):
        top = jnp.zeros((ROWS, LANES), F32)
        bottom = jnp.zeros((ROWS, LANES), F32)
        for z in range(depth):
            row = dens[z + 1, half, pl.ds(ROWS, 1), :]
            top = jnp.where(sub == z, jnp.broadcast_to(row, top.shape), top)
            row = dens[z + 1, half, pl.ds(height + ROWS - 1, 1), :]
            bottom = jnp.where(sub == z, jnp.broadcast_to(row, top.shape), bottom)
        rim[0, half] = top
        rim[1, half] = bottom
    x_up = remote(rim.at[1], rim_halo.at[0], 2, neighbours[1])
    x_down = remote(rim.at[0], rim_halo.at[1], 3, neighbours[0])

    @pl.when(me == 0)
    def _():
        for half in range(2):
            dens[0, half, pl.ds(ROWS, height), :] = jnp.zeros((height, LANES), F32)

    @pl.when(me == n_z - 1)
    def _():
        for half in range(2):
            dens[depth + 1, half, pl.ds(ROWS, height), :] = jnp.zeros(
                (height, LANES), F32
            )

    y_up = remote(edge.at[1], halo.at[0], 0, neighbours[3])
    y_down = remote(edge.at[0], halo.at[1], 1, neighbours[2])
    pl.semaphore_wait(barrier, len(neighbours) + 2 * reach)
    has_before = (gy > 0, gx > 0, me > 0)
    has_after = (gy < n_y - 1, gx < n_x - 1, me < n_z - 1)
    upward, downward = (y_up, x_up, z_up), (y_down, x_down, z_down)

    def sides(act, towards):
        for copies, there in zip((upward, downward), towards):
            for copy, here in zip(copies, there):
                pl.when(here)(functools.partial(act, copy))

    sides(lambda copy: copy.start(), (has_after, has_before))

    for sign in (-1, 1):
        pl.semaphore_signal(
            known,
            inc=1,
            device_id={"gz": step(me, n_z, sign * reach)},
            device_id_type=MESH,
        )

    def send_depth(by, carry):
        for sign in (-1, 1):
            depth_to(lax.rem(me + sign * by + n_z, n_z)).start()
        return carry

    lax.fori_loop(1, reach + 1, send_depth, 0)
    def tint(block, carry):
        rows = pl.ds(pl.multiple_of(block * ROWS, ROWS), ROWS)
        for z in range(depth):
            for half in range(2):
                bin_ = bins[z, half, rows, :]
                index, upper = bin_ & (LANES - 1), bin_ >= LANES
                for c in range(3):
                    tinted[c, z, half, rows, :] = weight[z, half, rows, :] * looked(
                        c, index, upper
                    )
        return carry

    lax.fori_loop(0, blocks, tint, 0)
    pl.semaphore_wait(known, 2)
    lax.fori_loop(reach + 1, n_z // 2, send_depth, 0)
    depth_to(lax.rem(me + n_z // 2, n_z)).start()

    sides(lambda copy: copy.wait_recv(), (has_before, has_after))

    blank = jnp.zeros((ROWS, LANES), F32)

    @pl.when(gx == 0)
    def _():
        for half in range(2):
            rim_halo[0, half] = blank

    @pl.when(gx == n_x - 1)
    def _():
        for half in range(2):
            rim_halo[1, half] = blank

    @pl.when(gy == 0)
    def _():
        halo[0] = blank

    @pl.when(gy == n_y - 1)
    def _():
        halo[1] = blank

    for half in range(2):
        before, after = rim_halo[0, half], rim_halo[1, half]
        for z in range(depth):
            dens[z + 1, half, pl.ds(ROWS - 1, 1), :] = before[z : z + 1, :]
            dens[z + 1, half, pl.ds(height + ROWS, 1), :] = after[z : z + 1, :]

    def colours(k, carry):
        block = jnp.where(me < n_z // 2, jnp.where(k < 2, k, jnp.where(k < 6, k + 2, k - 4)), jnp.where(me < n_z - n_z // 4, jnp.where(k < 2, k, jnp.where(k < 6, k + 2, k - 4)), k))
        rows = pl.ds(pl.multiple_of(block * ROWS, ROWS), ROWS)
        base = block * ROWS
        here = pl.ds(pl.multiple_of(base + ROWS, ROWS), ROWS)
        sums = [[jnp.zeros((ROWS, LANES), F32) for _ in range(2)] for _ in range(3)]
        for z in range(depth):
            low, high = dens[z + 1, 0, here, :], dens[z + 1, 1, here, :]
            column = z * blocks + block
            west = pltpu.roll(halo[0], LANES - column, 1)
            east = pltpu.roll(halo[1], LANES - 1 - column, 1)
            low_up, high_up = pltpu.roll(low, 1, 1), pltpu.roll(high, 1, 1)
            low_down = pltpu.roll(low, LANES - 1, 1)
            high_down = pltpu.roll(high, LANES - 1, 1)
            slopes_y = (
                jnp.where(lane == LANES - 1, high_down, low_down)
                - jnp.where(lane == 0, west, low_up),
                jnp.where(lane == LANES - 1, east, high_down)
                - jnp.where(lane == 0, low_up, high_up),
            )
            for half in range(2):
                slope_z = dens[z + 2, half, here, :] - dens[z, half, here, :]
                slope_x = (
                    dens[z + 1, half, pl.ds(base + ROWS + 1, ROWS), :]
                    - dens[z + 1, half, pl.ds(base + ROWS - 1, ROWS), :]
                )
                slope_y = slopes_y[half]
                facing = jnp.abs(0.48 * slope_z + 0.36 * slope_x + 0.45 * slope_y)
                square = (
                    slope_z * slope_z + slope_x * slope_x + slope_y * slope_y + 4.0
                )
                shade = 0.25 + facing * lax.rsqrt(square)
                for c in range(3):
                    sums[c][half] = sums[c][half] + shade * tinted[c, z, half, rows, :]
        for c in range(3):
            split(block, c, *sums[c])

        for other in (2 * block, 2 * block + 1):

            @pl.when(other != me)
            def _():
                colour_to(other).start()

        return carry

    lax.fori_loop(0, blocks, colours, 0)

    loads[6].wait()

    def place(rank, carry):
        slot = jnp.int32(0)
        for b in range(n_z):
            here = lax.rem(me + (n_z - b), n_z)
            slot = jnp.where(order_ref[0, 0, b] == rank, here, slot)
        inv[rank] = slot
        return carry

    lax.fori_loop(0, n_z, place, 0)

    recv[0] = send[me]

    others = pl.ds(1, n_z - 1)

    def all_tiles(channels, send_sem, recv_sem):
        return pltpu.make_async_remote_copy(
            src_ref=send.at[others, channels],
            dst_ref=recv.at[others, channels],
            send_sem=send_sem,
            recv_sem=recv_sem,
            device_id=above,
            device_id_type=MESH,
        )

    all_depths = all_tiles(3, depth_send, depth_recv)
    all_colours = all_tiles(pl.ds(0, 3), colour_send, colour_recv)
    all_depths.wait_recv()
    all_colours.wait_recv()

    ahead = jnp.zeros((ROWS, LANES), F32)
    image = [jnp.zeros((ROWS, LANES), F32) for _ in range(3)]
    for rank in range(n_z):
        slot = inv[rank]
        through = jnp.exp2(ahead)
        for c in range(3):
            image[c] = image[c] + through * recv[slot, c]
        ahead = ahead + recv[slot, 3]
    image.append(1.0 - jnp.exp2(ahead))
    for c in range(4):
        out_ref[c, :, 0:LANES] = image[c][0:4, :]
        out_ref[c, :, LANES : 2 * LANES] = image[c][4:8, :]

    sides(lambda copy: copy.wait_send(), (has_after, has_before))

    all_depths.wait_send()
    all_colours.wait_send()


def local(density, bins, colour_table, opacity_table, order):
    depth, height, width = density.shape
    n_z = lax.axis_size("gz")
    scale = -3.0 / (depth * n_z) * math.log2(math.e)
    vmem = pl.BlockSpec(memory_space=pltpu.VMEM)
    anywhere = pl.BlockSpec(memory_space=pl.ANY)
    return pl.pallas_call(
        functools.partial(kernel, n_z, scale),
        out_shape=pltpu.VMEM((4, height // n_z, width), F32),
        in_specs=[anywhere] * 5,
        out_specs=vmem,
        scratch_shapes=[
            pltpu.VMEM((depth + 2, 2, height + 2 * ROWS, LANES), F32),
            pltpu.VMEM((depth, 2, height, LANES), jnp.int32),
            pltpu.VMEM(colour_table.shape, colour_table.dtype),
            pltpu.VMEM(opacity_table.shape, opacity_table.dtype),
            pltpu.SMEM(order.shape, order.dtype),
            pltpu.VMEM((4, 2, ROWS, LANES), F32),
            pltpu.VMEM((depth, 2, height, LANES), F32),
            pltpu.VMEM((3, depth, 2, height, LANES), F32),
            pltpu.VMEM((2, ROWS, LANES), F32),
            pltpu.VMEM((2, ROWS, LANES), F32),
            pltpu.VMEM((2, 2, ROWS, LANES), F32),
            pltpu.VMEM((2, 2, ROWS, LANES), F32),
            pltpu.VMEM((n_z, 4, ROWS, LANES), F32),
            pltpu.VMEM((n_z, 4, ROWS, LANES), F32),
            pltpu.SMEM((n_z,), jnp.int32),
            pltpu.SemaphoreType.DMA((7,)),
            pltpu.SemaphoreType.DMA((6,)),
            pltpu.SemaphoreType.DMA((6,)),
            pltpu.SemaphoreType.DMA,
            pltpu.SemaphoreType.DMA,
            pltpu.SemaphoreType.DMA,
            pltpu.SemaphoreType.DMA,
            pltpu.SemaphoreType.REGULAR,
        ],
        compiler_params=pltpu.CompilerParams(collective_id=0, has_side_effects=True),
    )(density, bins, colour_table, opacity_table, order)


def solution(mesh):
    return jax.shard_map(
        local,
        mesh=mesh,
        in_specs=(
            P("gz", "gx", "gy"),
            P("gz", "gx", "gy"),
            P(),
            P(),
            P("gx", "gy", None),
        ),
        out_specs=P(None, ("gx", "gz"), "gy"),
        check_vma=False,
    )
```

```python
import functools
import math

import jax
import jax.numpy as jnp
from jax import lax
from jax.experimental import pallas as pl
from jax.experimental.pallas import tpu as pltpu
from jax.sharding import PartitionSpec as P

MESH = pl.DeviceIdType.MESH
LANES = 128
ROWS = 8
F32 = jnp.float32


def kernel(
    n_z,
    scale,
    dens_hbm,
    bins_hbm,
    ctab_hbm,
    otab_hbm,
    order_hbm,
    out_ref,
    dens,
    bins,
    ctab_ref,
    otab_ref,
    order_ref,
    tabs,
    weight,
    tinted,
    edge,
    halo,
    rim,
    rim_halo,
    send,
    recv,
    inv,
    load_sem,
    halo_send,
    halo_recv,
    depth_send,
    depth_recv,
    colour_send,
    colour_recv,
    known,
):
    gx, gy, me = lax.axis_index("gx"), lax.axis_index("gy"), lax.axis_index("gz")
    n_x, n_y = lax.axis_size("gx"), lax.axis_size("gy")
    depth, _, height, _ = bins.shape
    blocks = height // ROWS

    def step(index, count, by):
        return lax.rem(index + (by + count), count)

    neighbours = [
        {"gx": step(gx, n_x, -1)},
        {"gx": step(gx, n_x, 1)},
        {"gy": step(gy, n_y, -1)},
        {"gy": step(gy, n_y, 1)},
    ]
    below, above = {"gz": step(me, n_z, -1)}, {"gz": step(me, n_z, 1)}

    reach = n_z // 4
    barrier = pltpu.get_barrier_semaphore()

    def greet(by, carry):
        for sign in (-1, 1):
            pl.semaphore_signal(
                barrier,
                inc=1,
                device_id={"gz": lax.rem(me + sign * (reach - by) + n_z, n_z)},
                device_id_type=MESH,
            )
        return carry

    lax.fori_loop(0, reach, greet, 0)
    for other in neighbours:
        pl.semaphore_signal(barrier, inc=1, device_id=other, device_id_type=MESH)

    loads = []
    for half in range(2):
        lanes = pl.ds(half * LANES, LANES)
        loads.append(
            pltpu.make_async_copy(
                dens_hbm.at[:, :, lanes],
                dens.at[pl.ds(1, depth), half, pl.ds(ROWS, height), :],
                load_sem.at[0],
            )
        )
    for half in range(2):
        lanes = pl.ds(half * LANES, LANES)
        loads.append(
            pltpu.make_async_copy(
                bins_hbm.at[:, :, lanes], bins.at[:, half], load_sem.at[1]
            )
        )
    for index, (src, dst) in enumerate(
        ((ctab_hbm, ctab_ref), (otab_hbm, otab_ref), (order_hbm, order_ref))
    ):
        loads.append(pltpu.make_async_copy(src, dst, load_sem.at[2 + index]))
    for load in loads:
        load.start()
    loads[4].wait()
    loads[5].wait()

    table = jnp.concatenate(
        [ctab_ref[...].astype(F32), otab_ref[...].astype(F32).reshape(1, -1) * scale], axis=0
    )
    for c in range(4):
        for half in range(2):
            row = table[c : c + 1, half * LANES : (half + 1) * LANES]
            tabs[c, half] = jnp.broadcast_to(row, (ROWS, LANES))

    own = dens.at[pl.ds(1, depth), :, pl.ds(ROWS, height), :]
    pltpu.make_async_copy(own, own, load_sem.at[0]).wait()

    lane = lax.broadcasted_iota(jnp.int32, (ROWS, LANES), 1)
    sub = lax.broadcasted_iota(jnp.int32, (ROWS, LANES), 0)

    first = jnp.zeros((ROWS, LANES), F32)
    last = jnp.zeros((ROWS, LANES), F32)
    for z in range(depth):
        for b in range(blocks):
            k = z * blocks + b
            rows = pl.ds(ROWS + b * ROWS, ROWS)
            first = jnp.where(
                lane == k, jnp.broadcast_to(dens[z + 1, 0, rows, 0:1], first.shape), first
            )
            last = jnp.where(
                lane == k,
                jnp.broadcast_to(dens[z + 1, 1, rows, LANES - 1 : LANES], last.shape),
                last,
            )
    edge[0] = first
    edge[1] = last
    def split(block, channel, low, high):
        send[2 * block, channel] = jnp.where(sub < 4, low, pltpu.roll(high, 4, 0))
        send[2 * block + 1, channel] = jnp.where(sub < 4, pltpu.roll(low, 4, 0), high)

    def looked(c, index, upper):
        return jnp.where(
            upper,
            jnp.take_along_axis(tabs[c, 1], index, axis=1, mode="promise_in_bounds"),
            jnp.take_along_axis(tabs[c, 0], index, axis=1, mode="promise_in_bounds"),
        )

    pltpu.make_async_copy(bins, bins, load_sem.at[1]).wait()

    def optical(block, carry):
        rows = pl.ds(pl.multiple_of(block * ROWS, ROWS), ROWS)
        padded = pl.ds(pl.multiple_of(block * ROWS + ROWS, ROWS), ROWS)
        ends = []
        for half in range(2):
            total = jnp.zeros((ROWS, LANES), F32)
            before = jnp.ones((ROWS, LANES), F32)
            for z in range(depth):
                bin_ = bins[z, half, rows, :]
                sigma = looked(3, bin_ & (LANES - 1), bin_ >= LANES)
                total = total + sigma * dens[z + 1, half, padded, :]
                after = jnp.exp2(total)
                weight[z, half, rows, :] = before - after
                before = after
            ends.append(total)
        split(block, 3, *ends)
        return carry

    lax.fori_loop(0, blocks, optical, 0)

    def depth_to(other):
        slot = lax.rem(other - me + n_z, n_z)
        return pltpu.make_async_remote_copy(
            src_ref=send.at[other, 3],
            dst_ref=recv.at[slot, 3],
            send_sem=depth_send,
            recv_sem=depth_recv,
            device_id={"gz": other},
            device_id_type=MESH,
        )

    def colour_to(other):
        slot = lax.rem(other - me + n_z, n_z)
        return pltpu.make_async_remote_copy(
            src_ref=send.at[other, pl.ds(0, 3)],
            dst_ref=recv.at[slot, pl.ds(0, 3)],
            send_sem=colour_send,
            recv_sem=colour_recv,
            device_id={"gz": other},
            device_id_type=MESH,
        )

    def remote(src, dst, index, other):
        return pltpu.make_async_remote_copy(
            src_ref=src,
            dst_ref=dst,
            send_sem=halo_send.at[index],
            recv_sem=halo_recv.at[index],
            device_id=other,
            device_id_type=MESH,
        )

    rows = pl.ds(ROWS, height)
    z_up = remote(dens.at[depth, :, rows, :], dens.at[0, :, rows, :], 4, above)
    z_down = remote(dens.at[1, :, rows, :], dens.at[depth + 1, :, rows, :], 5, below)

    for half in range(2):
        top = jnp.zeros((ROWS, LANES), F32)
        bottom = jnp.zeros((ROWS, LANES), F32)
        for z in range(depth):
            row = dens[z + 1, half, pl.ds(ROWS, 1), :]
            top = jnp.where(sub == z, jnp.broadcast_to(row, top.shape), top)
            row = dens[z + 1, half, pl.ds(height + ROWS - 1, 1), :]
            bottom = jnp.where(sub == z, jnp.broadcast_to(row, top.shape), bottom)
        rim[0, half] = top
        rim[1, half] = bottom
    x_up = remote(rim.at[1], rim_halo.at[0], 2, neighbours[1])
    x_down = remote(rim.at[0], rim_halo.at[1], 3, neighbours[0])

    @pl.when(me == 0)
    def _():
        for half in range(2):
            dens[0, half, pl.ds(ROWS, height), :] = jnp.zeros((height, LANES), F32)

    @pl.when(me == n_z - 1)
    def _():
        for half in range(2):
            dens[depth + 1, half, pl.ds(ROWS, height), :] = jnp.zeros(
                (height, LANES), F32
            )

    y_up = remote(edge.at[1], halo.at[0], 0, neighbours[3])
    y_down = remote(edge.at[0], halo.at[1], 1, neighbours[2])
    pl.semaphore_wait(barrier, len(neighbours) + 2 * reach)
    has_before = (gy > 0, gx > 0, me > 0)
    has_after = (gy < n_y - 1, gx < n_x - 1, me < n_z - 1)
    upward, downward = (y_up, x_up, z_up), (y_down, x_down, z_down)

    def sides(act, towards):
        for copies, there in zip((upward, downward), towards):
            for copy, here in zip(copies, there):
                pl.when(here)(functools.partial(act, copy))

    for sign in (-1, 1):
        pl.semaphore_signal(
            known,
            inc=1,
            device_id={"gz": step(me, n_z, sign * reach)},
            device_id_type=MESH,
        )

    sides(lambda copy: copy.start(), (has_after, has_before))

    def send_depth(by, carry):
        for sign in (-1, 1):
            depth_to(lax.rem(me + sign * by + n_z, n_z)).start()
        return carry

    lax.fori_loop(1, reach + 1, send_depth, 0)
    def tint(block, carry):
        rows = pl.ds(pl.multiple_of(block * ROWS, ROWS), ROWS)
        for z in range(depth):
            for half in range(2):
                bin_ = bins[z, half, rows, :]
                index, upper = bin_ & (LANES - 1), bin_ >= LANES
                for c in range(3):
                    tinted[c, z, half, rows, :] = weight[z, half, rows, :] * looked(
                        c, index, upper
                    )
        return carry

    lax.fori_loop(0, blocks, tint, 0)
    pl.semaphore_wait(known, 2)
    lax.fori_loop(reach + 1, n_z // 2, send_depth, 0)
    depth_to(lax.rem(me + n_z // 2, n_z)).start()

    sides(lambda copy: copy.wait_recv(), (has_before, has_after))

    blank = jnp.zeros((ROWS, LANES), F32)

    @pl.when(gx == 0)
    def _():
        for half in range(2):
            rim_halo[0, half] = blank

    @pl.when(gx == n_x - 1)
    def _():
        for half in range(2):
            rim_halo[1, half] = blank

    @pl.when(gy == 0)
    def _():
        halo[0] = blank

    @pl.when(gy == n_y - 1)
    def _():
        halo[1] = blank

    for half in range(2):
        before, after = rim_halo[0, half], rim_halo[1, half]
        for z in range(depth):
            dens[z + 1, half, pl.ds(ROWS - 1, 1), :] = before[z : z + 1, :]
            dens[z + 1, half, pl.ds(height + ROWS, 1), :] = after[z : z + 1, :]

    def colours(k, carry):
        block = jnp.where(me < n_z // 2, jnp.where(k < 2, k, jnp.where(k < 6, k + 2, k - 4)), jnp.where(me < n_z - n_z // 4, jnp.where(k < 2, k, jnp.where(k < 6, k + 2, k - 4)), k))
        rows = pl.ds(pl.multiple_of(block * ROWS, ROWS), ROWS)
        base = block * ROWS
        here = pl.ds(pl.multiple_of(base + ROWS, ROWS), ROWS)
        sums = [[jnp.zeros((ROWS, LANES), F32) for _ in range(2)] for _ in range(3)]
        for z in range(depth):
            low, high = dens[z + 1, 0, here, :], dens[z + 1, 1, here, :]
            column = z * blocks + block
            west = pltpu.roll(halo[0], LANES - column, 1)
            east = pltpu.roll(halo[1], LANES - 1 - column, 1)
            low_up, high_up = pltpu.roll(low, 1, 1), pltpu.roll(high, 1, 1)
            low_down = pltpu.roll(low, LANES - 1, 1)
            high_down = pltpu.roll(high, LANES - 1, 1)
            slopes_y = (
                jnp.where(lane == LANES - 1, high_down, low_down)
                - jnp.where(lane == 0, west, low_up),
                jnp.where(lane == LANES - 1, east, high_down)
                - jnp.where(lane == 0, low_up, high_up),
            )
            for half in range(2):
                slope_z = dens[z + 2, half, here, :] - dens[z, half, here, :]
                slope_x = (
                    dens[z + 1, half, pl.ds(base + ROWS + 1, ROWS), :]
                    - dens[z + 1, half, pl.ds(base + ROWS - 1, ROWS), :]
                )
                slope_y = slopes_y[half]
                facing = jnp.abs(0.48 * slope_z + 0.36 * slope_x + 0.45 * slope_y)
                square = (
                    slope_z * slope_z + slope_x * slope_x + slope_y * slope_y + 4.0
                )
                shade = 0.25 + facing * lax.rsqrt(square)
                for c in range(3):
                    sums[c][half] = sums[c][half] + shade * tinted[c, z, half, rows, :]
        for c in range(3):
            split(block, c, *sums[c])

        for other in (2 * block, 2 * block + 1):

            @pl.when(other != me)
            def _():
                colour_to(other).start()

        return carry

    lax.fori_loop(0, blocks, colours, 0)

    loads[6].wait()

    def place(rank, carry):
        slot = jnp.int32(0)
        for b in range(n_z):
            here = lax.rem(me + (n_z - b), n_z)
            slot = jnp.where(order_ref[0, 0, b] == rank, here, slot)
        inv[rank] = slot
        return carry

    lax.fori_loop(0, n_z, place, 0)

    recv[0] = send[me]

    others = pl.ds(1, n_z - 1)

    def all_tiles(channels, send_sem, recv_sem):
        return pltpu.make_async_remote_copy(
            src_ref=send.at[others, channels],
            dst_ref=recv.at[others, channels],
            send_sem=send_sem,
            recv_sem=recv_sem,
            device_id=above,
            device_id_type=MESH,
        )

    all_depths = all_tiles(3, depth_send, depth_recv)
    all_colours = all_tiles(pl.ds(0, 3), colour_send, colour_recv)
    all_depths.wait_recv()
    all_colours.wait_recv()

    ahead = jnp.zeros((ROWS, LANES), F32)
    image = [jnp.zeros((ROWS, LANES), F32) for _ in range(3)]
    for rank in range(n_z):
        slot = inv[rank]
        through = jnp.exp2(ahead)
        for c in range(3):
            image[c] = image[c] + through * recv[slot, c]
        ahead = ahead + recv[slot, 3]
    image.append(1.0 - jnp.exp2(ahead))
    for c in range(4):
        out_ref[c, :, 0:LANES] = image[c][0:4, :]
        out_ref[c, :, LANES : 2 * LANES] = image[c][4:8, :]

    sides(lambda copy: copy.wait_send(), (has_after, has_before))

    all_depths.wait_send()
    all_colours.wait_send()


def local(density, bins, colour_table, opacity_table, order):
    depth, height, width = density.shape
    n_z = lax.axis_size("gz")
    scale = -3.0 / (depth * n_z) * math.log2(math.e)
    vmem = pl.BlockSpec(memory_space=pltpu.VMEM)
    anywhere = pl.BlockSpec(memory_space=pl.ANY)
    return pl.pallas_call(
        functools.partial(kernel, n_z, scale),
        out_shape=pltpu.VMEM((4, height // n_z, width), F32),
        in_specs=[anywhere] * 5,
        out_specs=vmem,
        scratch_shapes=[
            pltpu.VMEM((depth + 2, 2, height + 2 * ROWS, LANES), F32),
            pltpu.VMEM((depth, 2, height, LANES), jnp.int32),
            pltpu.VMEM(colour_table.shape, colour_table.dtype),
            pltpu.VMEM(opacity_table.shape, opacity_table.dtype),
            pltpu.SMEM(order.shape, order.dtype),
            pltpu.VMEM((4, 2, ROWS, LANES), F32),
            pltpu.VMEM((depth, 2, height, LANES), F32),
            pltpu.VMEM((3, depth, 2, height, LANES), F32),
            pltpu.VMEM((2, ROWS, LANES), F32),
            pltpu.VMEM((2, ROWS, LANES), F32),
            pltpu.VMEM((2, 2, ROWS, LANES), F32),
            pltpu.VMEM((2, 2, ROWS, LANES), F32),
            pltpu.VMEM((n_z, 4, ROWS, LANES), F32),
            pltpu.VMEM((n_z, 4, ROWS, LANES), F32),
            pltpu.SMEM((n_z,), jnp.int32),
            pltpu.SemaphoreType.DMA((5,)),
            pltpu.SemaphoreType.DMA((6,)),
            pltpu.SemaphoreType.DMA((6,)),
            pltpu.SemaphoreType.DMA,
            pltpu.SemaphoreType.DMA,
            pltpu.SemaphoreType.DMA,
            pltpu.SemaphoreType.DMA,
            pltpu.SemaphoreType.REGULAR,
        ],
        compiler_params=pltpu.CompilerParams(collective_id=0, has_side_effects=True),
    )(density, bins, colour_table, opacity_table, order)


def solution(mesh):
    return jax.shard_map(
        local,
        mesh=mesh,
        in_specs=(
            P("gz", "gx", "gy"),
            P("gz", "gx", "gy"),
            P(),
            P(),
            P("gx", "gy", None),
        ),
        out_specs=P(None, ("gx", "gz"), "gy"),
        check_vma=False,
    )
```

```python
import functools
import math

import jax
import jax.numpy as jnp
from jax import lax
from jax.experimental import pallas as pl
from jax.experimental.pallas import tpu as pltpu
from jax.sharding import PartitionSpec as P

MESH = pl.DeviceIdType.MESH
LANES = 128
ROWS = 8
F32 = jnp.float32


def kernel(
    n_z,
    scale,
    dens_hbm,
    bins_hbm,
    ctab_hbm,
    otab_hbm,
    order_hbm,
    out_ref,
    dens,
    bins,
    ctab_ref,
    otab_ref,
    order_ref,
    tabs,
    weight,
    tinted,
    edge,
    halo,
    rim,
    rim_halo,
    send,
    recv,
    inv,
    load_sem,
    halo_send,
    halo_recv,
    depth_send,
    depth_recv,
    colour_send,
    colour_recv,
    known,
):
    gx, gy, me = lax.axis_index("gx"), lax.axis_index("gy"), lax.axis_index("gz")
    n_x, n_y = lax.axis_size("gx"), lax.axis_size("gy")
    depth, _, height, _ = bins.shape
    blocks = height // ROWS

    def step(index, count, by):
        return lax.rem(index + (by + count), count)

    neighbours = [
        {"gx": step(gx, n_x, -1)},
        {"gx": step(gx, n_x, 1)},
        {"gy": step(gy, n_y, -1)},
        {"gy": step(gy, n_y, 1)},
    ]
    below, above = {"gz": step(me, n_z, -1)}, {"gz": step(me, n_z, 1)}

    reach = n_z // 4
    barrier = pltpu.get_barrier_semaphore()

    def greet(by, carry):
        for sign in (-1, 1):
            pl.semaphore_signal(
                barrier,
                inc=1,
                device_id={"gz": lax.rem(me + sign * (reach - by) + n_z, n_z)},
                device_id_type=MESH,
            )
        return carry

    lax.fori_loop(0, reach, greet, 0)
    for other in neighbours:
        pl.semaphore_signal(barrier, inc=1, device_id=other, device_id_type=MESH)

    loads = []
    for half in range(2):
        lanes = pl.ds(half * LANES, LANES)
        loads.append(
            pltpu.make_async_copy(
                dens_hbm.at[:, :, lanes],
                dens.at[pl.ds(1, depth), half, pl.ds(ROWS, height), :],
                load_sem.at[half],
            )
        )
    for half in range(2):
        lanes = pl.ds(half * LANES, LANES)
        loads.append(
            pltpu.make_async_copy(
                bins_hbm.at[:, :, lanes], bins.at[:, half], load_sem.at[2 + half]
            )
        )
    for index, (src, dst) in enumerate(
        ((ctab_hbm, ctab_ref), (otab_hbm, otab_ref), (order_hbm, order_ref))
    ):
        loads.append(pltpu.make_async_copy(src, dst, load_sem.at[4 + index]))
    for load in loads:
        load.start()
    loads[4].wait()
    loads[5].wait()

    table = jnp.concatenate(
        [ctab_ref[...].astype(F32), otab_ref[...].astype(F32).reshape(1, -1) * scale], axis=0
    )
    for c in range(4):
        for half in range(2):
            row = table[c : c + 1, half * LANES : (half + 1) * LANES]
            tabs[c, half] = jnp.broadcast_to(row, (ROWS, LANES))

    loads[0].wait()
    loads[1].wait()

    lane = lax.broadcasted_iota(jnp.int32, (ROWS, LANES), 1)
    sub = lax.broadcasted_iota(jnp.int32, (ROWS, LANES), 0)

    first = jnp.zeros((ROWS, LANES), F32)
    last = jnp.zeros((ROWS, LANES), F32)
    for z in range(depth):
        for b in range(blocks):
            k = z * blocks + b
            rows = pl.ds(ROWS + b * ROWS, ROWS)
            first = jnp.where(
                lane == k, jnp.broadcast_to(dens[z + 1, 0, rows, 0:1], first.shape), first
            )
            last = jnp.where(
                lane == k,
                jnp.broadcast_to(dens[z + 1, 1, rows, LANES - 1 : LANES], last.shape),
                last,
            )
    edge[0] = first
    edge[1] = last
    def split(block, channel, low, high):
        send[2 * block, channel] = jnp.where(sub < 4, low, pltpu.roll(high, 4, 0))
        send[2 * block + 1, channel] = jnp.where(sub < 4, pltpu.roll(low, 4, 0), high)

    def looked(c, index, upper):
        return jnp.where(
            upper,
            jnp.take_along_axis(tabs[c, 1], index, axis=1, mode="promise_in_bounds"),
            jnp.take_along_axis(tabs[c, 0], index, axis=1, mode="promise_in_bounds"),
        )

    loads[2].wait()
    loads[3].wait()

    def optical(block, carry):
        rows = pl.ds(pl.multiple_of(block * ROWS, ROWS), ROWS)
        padded = pl.ds(pl.multiple_of(block * ROWS + ROWS, ROWS), ROWS)
        ends = []
        for half in range(2):
            total = jnp.zeros((ROWS, LANES), F32)
            before = jnp.ones((ROWS, LANES), F32)
            for z in range(depth):
                bin_ = bins[z, half, rows, :]
                sigma = looked(3, bin_ & (LANES - 1), bin_ >= LANES)
                total = total + sigma * dens[z + 1, half, padded, :]
                after = jnp.exp2(total)
                weight[z, half, rows, :] = before - after
                before = after
            ends.append(total)
        split(block, 3, *ends)
        return carry

    lax.fori_loop(0, blocks, optical, 0)

    def depth_to(other):
        slot = lax.rem(other - me + n_z, n_z)
        return pltpu.make_async_remote_copy(
            src_ref=send.at[other, 3],
            dst_ref=recv.at[slot, 3],
            send_sem=depth_send,
            recv_sem=depth_recv,
            device_id={"gz": other},
            device_id_type=MESH,
        )

    def colour_to(other):
        slot = lax.rem(other - me + n_z, n_z)
        return pltpu.make_async_remote_copy(
            src_ref=send.at[other, pl.ds(0, 3)],
            dst_ref=recv.at[slot, pl.ds(0, 3)],
            send_sem=colour_send,
            recv_sem=colour_recv,
            device_id={"gz": other},
            device_id_type=MESH,
        )

    def remote(src, dst, index, other):
        return pltpu.make_async_remote_copy(
            src_ref=src,
            dst_ref=dst,
            send_sem=halo_send.at[index],
            recv_sem=halo_recv.at[index],
            device_id=other,
            device_id_type=MESH,
        )

    rows = pl.ds(ROWS, height)
    z_up = remote(dens.at[depth, :, rows, :], dens.at[0, :, rows, :], 4, above)
    z_down = remote(dens.at[1, :, rows, :], dens.at[depth + 1, :, rows, :], 5, below)

    for half in range(2):
        top = jnp.zeros((ROWS, LANES), F32)
        bottom = jnp.zeros((ROWS, LANES), F32)
        for z in range(depth):
            row = dens[z + 1, half, pl.ds(ROWS, 1), :]
            top = jnp.where(sub == z, jnp.broadcast_to(row, top.shape), top)
            row = dens[z + 1, half, pl.ds(height + ROWS - 1, 1), :]
            bottom = jnp.where(sub == z, jnp.broadcast_to(row, top.shape), bottom)
        rim[0, half] = top
        rim[1, half] = bottom
    x_up = remote(rim.at[1], rim_halo.at[0], 2, neighbours[1])
    x_down = remote(rim.at[0], rim_halo.at[1], 3, neighbours[0])

    @pl.when(me == 0)
    def _():
        for half in range(2):
            dens[0, half, pl.ds(ROWS, height), :] = jnp.zeros((height, LANES), F32)

    @pl.when(me == n_z - 1)
    def _():
        for half in range(2):
            dens[depth + 1, half, pl.ds(ROWS, height), :] = jnp.zeros(
                (height, LANES), F32
            )

    y_up = remote(edge.at[1], halo.at[0], 0, neighbours[3])
    y_down = remote(edge.at[0], halo.at[1], 1, neighbours[2])
    pl.semaphore_wait(barrier, len(neighbours) + 2 * reach)
    has_before = (gy > 0, gx > 0, me > 0)
    has_after = (gy < n_y - 1, gx < n_x - 1, me < n_z - 1)
    upward, downward = (y_up, x_up, z_up), (y_down, x_down, z_down)

    def sides(act, towards):
        for copies, there in zip((upward, downward), towards):
            for copy, here in zip(copies, there):
                pl.when(here)(functools.partial(act, copy))

    sides(lambda copy: copy.start(), (has_after, has_before))

    for sign in (-1, 1):
        pl.semaphore_signal(
            known,
            inc=1,
            device_id={"gz": step(me, n_z, sign * reach)},
            device_id_type=MESH,
        )

    def send_depth(by, carry):
        for sign in (-1, 1):
            depth_to(lax.rem(me + sign * by + n_z, n_z)).start()
        return carry

    lax.fori_loop(1, reach + 1, send_depth, 0)
    def tint(block, carry):
        rows = pl.ds(pl.multiple_of(block * ROWS, ROWS), ROWS)
        for z in range(depth):
            for half in range(2):
                bin_ = bins[z, half, rows, :]
                index, upper = bin_ & (LANES - 1), bin_ >= LANES
                for c in range(3):
                    tinted[c, z, half, rows, :] = weight[z, half, rows, :] * looked(
                        c, index, upper
                    )
        return carry

    lax.fori_loop(0, blocks, tint, 0)
    pl.semaphore_wait(known, 2)
    lax.fori_loop(reach + 1, n_z // 2, send_depth, 0)
    depth_to(lax.rem(me + n_z // 2, n_z)).start()

    sides(lambda copy: copy.wait_recv(), (has_before, has_after))

    blank = jnp.zeros((ROWS, LANES), F32)

    @pl.when(gx == 0)
    def _():
        for half in range(2):
            rim_halo[0, half] = blank

    @pl.when(gx == n_x - 1)
    def _():
        for half in range(2):
            rim_halo[1, half] = blank

    @pl.when(gy == 0)
    def _():
        halo[0] = blank

    @pl.when(gy == n_y - 1)
    def _():
        halo[1] = blank

    for half in range(2):
        before, after = rim_halo[0, half], rim_halo[1, half]
        for z in range(depth):
            dens[z + 1, half, pl.ds(ROWS - 1, 1), :] = before[z : z + 1, :]
            dens[z + 1, half, pl.ds(height + ROWS, 1), :] = after[z : z + 1, :]

    def colours(k, carry):
        block = jnp.where(me < n_z // 2, jnp.where(k < 2, k, jnp.where(k < 6, k + 2, k - 4)), jnp.where(me < n_z - n_z // 4, jnp.where(k < 2, k, jnp.where(k < 6, k + 2, k - 4)), jnp.where(k < 4, k, 11 - k)))
        rows = pl.ds(pl.multiple_of(block * ROWS, ROWS), ROWS)
        base = block * ROWS
        here = pl.ds(pl.multiple_of(base + ROWS, ROWS), ROWS)
        sums = [[jnp.zeros((ROWS, LANES), F32) for _ in range(2)] for _ in range(3)]
        for z in range(depth):
            low, high = dens[z + 1, 0, here, :], dens[z + 1, 1, here, :]
            column = z * blocks + block
            west = pltpu.roll(halo[0], LANES - column, 1)
            east = pltpu.roll(halo[1], LANES - 1 - column, 1)
            low_up, high_up = pltpu.roll(low, 1, 1), pltpu.roll(high, 1, 1)
            low_down = pltpu.roll(low, LANES - 1, 1)
            high_down = pltpu.roll(high, LANES - 1, 1)
            slopes_y = (
                jnp.where(lane == LANES - 1, high_down, low_down)
                - jnp.where(lane == 0, west, low_up),
                jnp.where(lane == LANES - 1, east, high_down)
                - jnp.where(lane == 0, low_up, high_up),
            )
            for half in range(2):
                slope_z = dens[z + 2, half, here, :] - dens[z, half, here, :]
                slope_x = (
                    dens[z + 1, half, pl.ds(base + ROWS + 1, ROWS), :]
                    - dens[z + 1, half, pl.ds(base + ROWS - 1, ROWS), :]
                )
                slope_y = slopes_y[half]
                facing = jnp.abs(0.48 * slope_z + 0.36 * slope_x + 0.45 * slope_y)
                square = (
                    slope_z * slope_z + slope_x * slope_x + slope_y * slope_y + 4.0
                )
                shade = 0.25 + facing * lax.rsqrt(square)
                for c in range(3):
                    sums[c][half] = sums[c][half] + shade * tinted[c, z, half, rows, :]
        for c in range(3):
            split(block, c, *sums[c])

        for other in (2 * block, 2 * block + 1):

            @pl.when(other != me)
            def _():
                colour_to(other).start()

        return carry

    lax.fori_loop(0, blocks, colours, 0)

    loads[6].wait()

    def place(rank, carry):
        slot = jnp.int32(0)
        for b in range(n_z):
            here = lax.rem(me + (n_z - b), n_z)
            slot = jnp.where(order_ref[0, 0, b] == rank, here, slot)
        inv[rank] = slot
        return carry

    lax.fori_loop(0, n_z, place, 0)

    recv[0] = send[me]

    others = pl.ds(1, n_z - 1)

    def all_tiles(channels, send_sem, recv_sem):
        return pltpu.make_async_remote_copy(
            src_ref=send.at[others, channels],
            dst_ref=recv.at[others, channels],
            send_sem=send_sem,
            recv_sem=recv_sem,
            device_id=above,
            device_id_type=MESH,
        )

    all_depths = all_tiles(3, depth_send, depth_recv)
    all_colours = all_tiles(pl.ds(0, 3), colour_send, colour_recv)
    all_depths.wait_recv()
    all_colours.wait_recv()

    ahead = jnp.zeros((ROWS, LANES), F32)
    image = [jnp.zeros((ROWS, LANES), F32) for _ in range(3)]
    for rank in range(n_z):
        slot = inv[rank]
        through = jnp.exp2(ahead)
        for c in range(3):
            image[c] = image[c] + through * recv[slot, c]
        ahead = ahead + recv[slot, 3]
    image.append(1.0 - jnp.exp2(ahead))
    for c in range(4):
        out_ref[c, :, 0:LANES] = image[c][0:4, :]
        out_ref[c, :, LANES : 2 * LANES] = image[c][4:8, :]

    sides(lambda copy: copy.wait_send(), (has_after, has_before))

    all_depths.wait_send()
    all_colours.wait_send()


def local(density, bins, colour_table, opacity_table, order):
    depth, height, width = density.shape
    n_z = lax.axis_size("gz")
    scale = -3.0 / (depth * n_z) * math.log2(math.e)
    vmem = pl.BlockSpec(memory_space=pltpu.VMEM)
    anywhere = pl.BlockSpec(memory_space=pl.ANY)
    return pl.pallas_call(
        functools.partial(kernel, n_z, scale),
        out_shape=pltpu.VMEM((4, height // n_z, width), F32),
        in_specs=[anywhere] * 5,
        out_specs=vmem,
        scratch_shapes=[
            pltpu.VMEM((depth + 2, 2, height + 2 * ROWS, LANES), F32),
            pltpu.VMEM((depth, 2, height, LANES), jnp.int32),
            pltpu.VMEM(colour_table.shape, colour_table.dtype),
            pltpu.VMEM(opacity_table.shape, opacity_table.dtype),
            pltpu.SMEM(order.shape, order.dtype),
            pltpu.VMEM((4, 2, ROWS, LANES), F32),
            pltpu.VMEM((depth, 2, height, LANES), F32),
            pltpu.VMEM((3, depth, 2, height, LANES), F32),
            pltpu.VMEM((2, ROWS, LANES), F32),
            pltpu.VMEM((2, ROWS, LANES), F32),
            pltpu.VMEM((2, 2, ROWS, LANES), F32),
            pltpu.VMEM((2, 2, ROWS, LANES), F32),
            pltpu.VMEM((n_z, 4, ROWS, LANES), F32),
            pltpu.VMEM((n_z, 4, ROWS, LANES), F32),
            pltpu.SMEM((n_z,), jnp.int32),
            pltpu.SemaphoreType.DMA((7,)),
            pltpu.SemaphoreType.DMA((6,)),
            pltpu.SemaphoreType.DMA((6,)),
            pltpu.SemaphoreType.DMA,
            pltpu.SemaphoreType.DMA,
            pltpu.SemaphoreType.DMA,
            pltpu.SemaphoreType.DMA,
            pltpu.SemaphoreType.REGULAR,
        ],
        compiler_params=pltpu.CompilerParams(collective_id=0, has_side_effects=True),
    )(density, bins, colour_table, opacity_table, order)


def solution(mesh):
    return jax.shard_map(
        local,
        mesh=mesh,
        in_specs=(
            P("gz", "gx", "gy"),
            P("gz", "gx", "gy"),
            P(),
            P(),
            P("gx", "gy", None),
        ),
        out_specs=P(None, ("gx", "gz"), "gy"),
        check_vma=False,
    )
```
